32 devices in a mesh: branch: 8 (over z, core), tensor: 4 (over y, x).
Axes of the slice: x: 2, y: 2, z: 4, core: 2. Of those that a mesh axis runs over, the one named last changes fastest.
Arguments:
- queries: bfloat16 [3072, 8192], P('branch', 'tensor'), may hold values from -5 to 5
- new_kv: bfloat16 [3072, 8, 256], P('branch'), may hold values from -5 to 5
- cache: bfloat16 [256, 128, 2048], P('branch', 'tensor'), may hold values from -5 to 5
- parents: int32 [8, 48], replicated, may hold values from 0 to 255, as said below
- depth: int32 [8, 3], P('branch'), may hold values from 1 to 48, as said below
Outputs:
- attended: bfloat16 [3072, 8192], P('branch', 'tensor')
The draws below stay inside these ranges and needn't reach their ends.
Inputs may be any that keep to these rules, and one draw needn't show every extreme that they name: `parents`: each row names 48 distinct blocks; block b is held by branch index b // 32. At most 9 entries of one row are held by one branch index, and in every row some branch index holds exactly 9 of them. `depth`: some node of some group reads its whole list.
All inputs are finite; a program needn't handle non-finite values.
Results may differ from the reference program's by a relative error of at most 0.0055.
Values may be sent and summed in bfloat16 or wider, within the bound.
A program may use at most 64 MiB of HBM per device.

```python
import math
import jax
import jax.numpy as jnp
from jax import lax

HQ = 64
KVH = 8
HD = 128
BT = 128
NODE_TOK = 128
NODES = 3
P_SIZE = 48
BLOCKS = 256
BLK_DEV = 32
CAP = 9
NEW = 384
TOKENS = 3072
N_BRANCH = 8


def draw_parents(key, part):

    def one_group(group):
        group_key = jax.random.fold_in(jax.random.fold_in(key, 11), group)
        owners = jax.random.permutation(jax.random.fold_in(group_key, 1), N_BRANCH)

        def local_pick(owner_slot):
            return jax.random.permutation(jax.random.fold_in(jax.random.fold_in(group_key, 2), owner_slot), BLK_DEV)[:CAP]
        table = jax.vmap(local_pick)(jnp.arange(N_BRANCH))
        slot_ids = jnp.arange(P_SIZE)
        stretch_ids = slot_ids // CAP
        picked = owners[stretch_ids] * BLK_DEV + table[stretch_ids, slot_ids % CAP]
        shuffle = jax.random.permutation(jax.random.fold_in(group_key, 3), P_SIZE)
        return picked[shuffle]
    return jax.vmap(one_group)(jnp.arange(N_BRANCH)).astype(jnp.int32)


def draw_depth(key, part):
    base_key = jax.random.fold_in(key, 23)
    tiers = jax.random.randint(jax.random.fold_in(base_key, 1), (N_BRANCH, 1), 1, 5)
    base_depth = jax.random.randint(jax.random.fold_in(base_key, 2), (N_BRANCH, NODES), 1, P_SIZE // 4 + 1)
    depths = jnp.minimum(base_depth * tiers, P_SIZE)
    full_group = jax.random.randint(jax.random.fold_in(base_key, 3), (), 0, N_BRANCH)
    full_node = jax.random.randint(jax.random.fold_in(base_key, 4), (), 0, NODES)
    is_full = (jnp.arange(N_BRANCH)[:, None] == full_group) & (jnp.arange(NODES)[None, :] == full_node)
    return jnp.where(is_full, P_SIZE, depths).astype(jnp.int32)


def draw_queries(key, part):
    base_key = jax.random.fold_in(key, 31)
    values = jnp.clip(jax.random.normal(jax.random.fold_in(base_key, 1), (TOKENS, HQ * HD), jnp.float32), -5.0, 5.0)
    return values.astype(jnp.bfloat16)


def draw_new_kv(key, part):
    base_key = jax.random.fold_in(key, 41)
    values = jnp.clip(jax.random.normal(jax.random.fold_in(base_key, 1), (TOKENS, KVH, 2 * HD), jnp.float32), -5.0, 5.0)
    return values.astype(jnp.bfloat16)


def steps_of(rng, shape, cuts, low, high):
    def one(axis_at, blocks):
        steps = jax.random.uniform(jax.random.fold_in(jax.random.fold_in(rng, 6), axis_at), (blocks,), jnp.float32, low / len(cuts), high / len(cuts))
        return jnp.repeat(jnp.exp(steps), shape[axis_at] // blocks).reshape((-1,) + (1,) * (len(shape) - axis_at - 1))

    gain = one(*cuts[0])
    for cut in cuts[1:]:
        gain = gain * one(*cut)
    return gain


def scatter_about(rng, shape, scale, limit, split=(), dtype=jnp.bfloat16):
    array = jax.random.normal(rng, shape, jnp.float32) * scale
    if len(split) > 0:
        array = steps_of(rng, shape, split, -0.22, 0.18) * array
    return jnp.clip(array, min=-limit, max=limit).astype(dtype)


def setup_inputs(seed: int = 0) -> dict:
    seeds = jax.random.split(jax.random.key(seed), 6)
    return {
        "queries": draw_queries(jax.random.fold_in(seeds[5], 71), 0),
        "new_kv": draw_new_kv(jax.random.fold_in(seeds[5], 71), 0),
        "cache": scatter_about(seeds[2], (BLOCKS, BT, KVH * 2 * HD), 1.0, 5.0, ((0, 8), (1, 4))),
        "parents": draw_parents(jax.random.fold_in(seeds[5], 71), 0),
        "depth": draw_depth(jax.random.fold_in(seeds[5], 71), 0),
    }


def reference(queries, new_kv, cache, parents, depth):
    sharing = HQ // KVH
    score_scale = 1.0 / math.sqrt(HD)
    positions = jnp.arange(NEW)
    node_of = positions // NODE_TOK
    causal = (node_of[:, None] == node_of[None, :]) & (positions[None, :] <= positions[:, None])
    anc_slot = jnp.arange(P_SIZE * BT) // BT

    def one_group(group):
        start = (group * NEW).astype(jnp.int32)
        q_heads = lax.dynamic_slice_in_dim(queries, start, NEW, 0).reshape(NEW, KVH, sharing, HD)
        fresh_kv = lax.dynamic_slice_in_dim(new_kv, start, NEW, 0)
        own_row = parents[group]
        ancestry = jnp.take(cache, own_row, axis=0).reshape(P_SIZE * BT, KVH, 2 * HD)
        keys_all = jnp.concatenate([ancestry, fresh_kv], axis=0)
        seen_depth = depth[group][node_of]
        anc_visible = anc_slot[None, :] < seen_depth[:, None]
        visible = jnp.concatenate([anc_visible, causal], axis=1)

        def one_head(head):
            q_part = q_heads[:, head].astype(jnp.float32)
            k_part = keys_all[:, head, :HD].astype(jnp.float32)
            v_part = keys_all[:, head, HD:].astype(jnp.float32)
            scores = jnp.einsum('rbd,kd->brk', q_part, k_part) * score_scale
            scores = jnp.where(visible[None], scores, -jnp.inf)
            row_peak = lax.optimization_barrier(jnp.max(scores, axis=-1, keepdims=True))
            weights = jnp.exp(scores - row_peak)
            row_total = lax.optimization_barrier(jnp.sum(weights, axis=-1))
            rounded = lax.optimization_barrier(weights.astype(jnp.bfloat16)).astype(jnp.float32)
            summed = jnp.einsum('brk,kd->rbd', rounded, v_part)
            return (summed / row_total.T[:, :, None]).astype(jnp.bfloat16)
        per_head = lax.map(one_head, jnp.arange(KVH))
        return jnp.transpose(per_head, (1, 0, 2, 3)).reshape(NEW, HQ * HD)
    groups_out = lax.map(one_group, jnp.arange(N_BRANCH))
    return groups_out.reshape(N_BRANCH * NEW, HQ * HD)
```

```python
import functools
import math

import jax
import jax.numpy as jnp
from jax import lax
from jax.experimental import pallas as pl
from jax.experimental.pallas import tpu as pltpu
from jax.sharding import PartitionSpec as P

HQ = 64
KVH = 8
HD = 128
BT = 128
NODE_TOK = 128
P_SIZE = 48
STEP_BLOCKS = 4
K = 2
LAG = 3
RING = 4
LEVELS = (24, 26, 28, 30, 34, 42)
MESH = pl.DeviceIdType.MESH


def plan(zs, blk_dev, region, levels, parents, deep, me):
    n = 2 * zs
    nb = n * blk_dev
    big = 1 << 20
    i32 = jnp.int32
    lane = lax.broadcasted_iota(i32, (n, 128), 1)
    act = jnp.where(lane < deep, parents, -1)
    blk = lax.broadcasted_iota(i32, (nb, 128), 0)
    need = []
    for z in range(zs):
        hit = (act[2 * z : 2 * z + 1, :] == blk) | (act[2 * z + 1 : 2 * z + 2, :] == blk)
        need.append(jnp.max(jnp.where(hit, 1, 0), axis=1, keepdims=True) > 0)
    bcol = lax.broadcasted_iota(i32, (nb, 1), 0)
    owner = jnp.zeros((nb, 1), i32)
    for o in range(1, n):
        owner = owner + jnp.where(bcol >= o * blk_dev, 1, 0)
    zb = owner >> 1
    cb = owner & 1
    eye = lax.broadcasted_iota(i32, (nb, nb), 0) == lax.broadcasted_iota(i32, (nb, nb), 1)

    def row(x):
        return jnp.sum(jnp.where(eye, x, 0), axis=0, keepdims=True)

    def rank(key):
        return jnp.sum(jnp.where(row(key) < key, 1, 0), axis=1, keepdims=True)

    def direction(fwd):
        zc = zb if fwd else zs - 1 - zb
        far = jnp.full((nb, 1), -1, i32)
        for z in range(zs):
            zz = z if fwd else zs - 1 - z
            far = jnp.where(need[z] & (zz > zc), jnp.maximum(far, zz), far)
        own_rank = jnp.full((nb, 1), big, i32)
        slots = []
        total = jnp.zeros((1, 1), i32)
        prev = jnp.zeros((nb, 1), i32)
        for k in range(zs - 1):
            own = (zc == k) & (far > k)
            rel = (zc < k) & (far > k)
            first = (cb * zs + (zs - far)) * nb + bcol
            key = jnp.where(own, first, jnp.where(rel, big + prev, 2 * big + bcol))
            key_row = row(key)
            r0 = jnp.sum(jnp.where(key_row < key, 1, 0), axis=1, keepdims=True)
            n0 = jnp.sum(jnp.where(own & (cb == 0), 1, 0), axis=0, keepdims=True)
            n1 = jnp.sum(jnp.where(own & (cb == 1), 1, 0), axis=0, keepdims=True)
            top = jnp.maximum(n0, n1)
            short = jnp.where(n0 <= n1, 0, 1)
            mine = r0 - cb * n0
            if k > 0:
                ready = (prev >> (K.bit_length())) + LAG
                at = jnp.where(ready * K <= top, top + ready * K, 2 * K * ready)
                gap_row = row(jnp.where(rel, at - r0, -big))
                gap = jnp.max(jnp.where(key_row <= key, gap_row, -big), axis=1, keepdims=True)
                r = r0 + jnp.maximum(gap, 0)
            else:
                r = r0
            far_slot = jnp.where(r < 2 * top, 2 * (r - top) + short, r)
            q = jnp.where(own, 2 * mine + cb, jnp.where(rel, far_slot, -1))
            own_rank = jnp.where(own, mine, own_rank)
            total = jnp.maximum(total, jnp.max(q, axis=0, keepdims=True) + 1)
            slots.append(q)
            prev = jnp.maximum(q, 0)
        return slots, own_rank, total

    right, rank_r, total_r = direction(True)
    left, rank_l, total_l = direction(False)
    local = jnp.zeros((nb, 1), jnp.bool_)
    for z in range(zs):
        local = local | (need[z] & (zb == z))
    key = jnp.minimum(2 * rank_r, 2 * rank_l + 1)
    key = jnp.where(key < big, key, jnp.where(local, big // 2 + bcol, big + bcol))
    order = rank(owner * (4 * big) + key) - owner * blk_dev

    me_z = me // 2
    me_c = me % 2
    lanes = lax.broadcasted_iota(i32, (1, 128), 1)

    def table(where_col, value_col):
        return jnp.sum(jnp.where(where_col == lanes, value_col, 0), axis=0, keepdims=True)

    def pick_link(slots, k):
        q = jnp.full((nb, 1), -1, i32)
        for j in range(zs - 1):
            q = jnp.where(k == j, slots[j], q)
        return q

    mine = owner == me
    picks = table(jnp.where(mine, order, -1), bcol - owner * blk_dev)

    def sources(slots, k):
        q = pick_link(slots, k)
        came = pick_link(slots, k - 1)
        source = jnp.where(zb == me_z, order, blk_dev + came)
        use = (q >= 0) & ((q & 1) == me_c)
        return table(jnp.where(use, q >> 1, -1), source)

    sel_r = sources(right, me_z)
    sel_l = sources(left, zs - 1 - me_z)
    from_r = pick_link(right, me_z - 1)
    from_l = pick_link(left, zs - 2 - me_z)
    place = jnp.where(
        zb == me_z,
        2 * order + cb,
        jnp.where(zb < me_z, 2 * blk_dev + from_r, 2 * (blk_dev + region) + from_l),
    )
    slot_count = (jnp.maximum(total_r, total_l) + 1) >> 1
    choice = jnp.zeros((1, 1), i32)
    for c in levels:
        choice = choice + jnp.where(slot_count > c, 1, 0)
    place = jnp.where(choice == len(levels), bcol, place)
    groups = lax.broadcasted_iota(i32, (n, 128), 0)
    my_row = jnp.sum(jnp.where(groups == me, act, 0), axis=0, keepdims=True)
    last = jnp.sum(jnp.where((groups == me) & (lane == deep - 1), act, 0), axis=(0, 1), keepdims=True)
    my_row = jnp.where(my_row < 0, last, my_row)
    pos = jnp.sum(jnp.where(bcol == my_row, place, 0), axis=0, keepdims=True)
    return picks, sel_r, sel_l, pos, choice, slot_count


def plan_kernel(zs, blk_dev, region, parents_ref, mine_ref, table_ref, all_ref, send_sem, recv_sem):
    n = 2 * zs
    me = lax.axis_index("branch")
    barrier = pltpu.get_barrier_semaphore()

    def greet(i, carry):
        peer = lax.rem(me + i, n)
        pl.semaphore_signal(barrier, inc=1, device_id={"branch": peer}, device_id_type=MESH)
        return carry

    lax.fori_loop(1, n, greet, 0)
    pl.semaphore_wait(barrier, n - 1)

    def copy(i):
        return pltpu.make_async_remote_copy(
            src_ref=mine_ref,
            dst_ref=all_ref.at[me],
            send_sem=send_sem.at[i],
            recv_sem=recv_sem.at[i],
            device_id={"branch": lax.rem(me + i, n)},
            device_id_type=MESH,
        )

    def start(i, carry):
        copy(i).start()
        return carry

    def finish(i, carry):
        copy(i).wait()
        return carry

    lax.fori_loop(1, n, start, 0)
    all_ref[pl.ds(me, 1)] = mine_ref[...][None]
    lax.fori_loop(1, n, finish, 0)
    deep = jnp.concatenate([jnp.max(all_ref[g, 0:1, :], axis=1, keepdims=True) for g in range(n)], axis=0)
    picks, sel_r, sel_l, pos, choice, _ = plan(
        zs, blk_dev, region, LEVELS, parents_ref[...], deep, me
    )
    wide = jnp.broadcast_to(choice, (1, 128))
    table_ref[...] = jnp.concatenate(
        [picks, sel_r, sel_l, pos, wide, mine_ref[0:1, :], wide, wide], axis=0
    )


def make_plan(parents, depth, n, blk_dev, region):
    nodes = depth.shape[1]
    mine = jnp.zeros((8, 128), jnp.int32) + jnp.pad(depth, ((0, 0), (0, 128 - nodes)))
    listed = jnp.pad(parents, ((0, 0), (0, 128 - parents.shape[1])), constant_values=-1)
    return pl.pallas_call(
        functools.partial(plan_kernel, n // 2, blk_dev, region),
        out_shape=jax.ShapeDtypeStruct((8, 128), jnp.int32),
        in_specs=[pl.BlockSpec(memory_space=pltpu.VMEM)] * 2,
        out_specs=pl.BlockSpec(memory_space=pltpu.VMEM),
        scratch_shapes=[
            pltpu.VMEM((n, 8, 128), jnp.int32),
            pltpu.SemaphoreType.DMA((n,)),
            pltpu.SemaphoreType.DMA((n,)),
        ],
        compiler_params=pltpu.CompilerParams(collective_id=0, has_side_effects=True),
    )(listed, mine)


def pack_kernel(first_cols, width, pick_ref, block_ref, packed_ref):
    for t, first in enumerate(first_cols):
        packed_ref[t, 0] = block_ref[0, :, first : first + width]


def pack(cache, picks, count, first_cols, width):
    rows = cache.shape[1]
    tensors = len(first_cols)
    return pl.pallas_call(
        functools.partial(pack_kernel, first_cols, width),
        out_shape=jax.ShapeDtypeStruct((tensors, count, rows, width), cache.dtype),
        grid_spec=pltpu.PrefetchScalarGridSpec(
            num_scalar_prefetch=1,
            grid=(count,),
            in_specs=[pl.BlockSpec((1, rows, cache.shape[2]), lambda i, pick: (pick[i], 0, 0))],
            out_specs=pl.BlockSpec((tensors, 1, rows, width), lambda i, pick: (0, i, 0, 0)),
        ),
    )(picks, cache)


def spread_kernel(branches, tensors, count, chunk, packed_ref, out_ref, tp_send, tp_recv, own_sem,
                  right_send, right_recv, left_send, left_recv, pair_send, pair_recv):
    me_b = lax.axis_index("branch")
    me_t = lax.axis_index("tensor")
    z = me_b // 2
    depth_z = branches // 2
    partner = me_b + 1 - 2 * (me_b % 2)
    chunks = count // chunk
    has_left = z > 0
    has_right = z < depth_z - 1
    barrier = pltpu.get_barrier_semaphore()
    for step in range(1, tensors):
        pl.semaphore_signal(
            barrier, inc=1, device_id={"tensor": lax.rem(me_t + step, tensors)}, device_id_type=MESH
        )
    pl.semaphore_signal(barrier, inc=1, device_id={"branch": partner}, device_id_type=MESH)

    @pl.when(has_left)
    def _():
        pl.semaphore_signal(barrier, inc=1, device_id={"branch": me_b - 2}, device_id_type=MESH)

    @pl.when(has_right)
    def _():
        pl.semaphore_signal(barrier, inc=1, device_id={"branch": me_b + 2}, device_id_type=MESH)

    pl.semaphore_wait(barrier, tensors + jnp.minimum(z, 1) + jnp.minimum(depth_z - 1 - z, 1))

    def span(c):
        return pl.ds(c * chunk, chunk)

    def tensor_copy(step, c):
        to = lax.rem(me_t + step, tensors)
        return pltpu.make_async_remote_copy(
            src_ref=packed_ref.at[to, span(c)],
            dst_ref=out_ref.at[me_b, span(c), me_t],
            send_sem=tp_send.at[step - 1, c],
            recv_sem=tp_recv.at[step - 1, c],
            device_id={"tensor": to},
            device_id_type=MESH,
        )

    def own_copy(c):
        return pltpu.make_async_copy(
            packed_ref.at[me_t, span(c)], out_ref.at[me_b, span(c), me_t], own_sem.at[c]
        )

    def lane_copy(origin, c, target, send_sem, recv_sem):
        return pltpu.make_async_remote_copy(
            src_ref=out_ref.at[origin, span(c)],
            dst_ref=out_ref.at[origin, span(c)],
            send_sem=send_sem,
            recv_sem=recv_sem,
            device_id={"branch": target},
            device_id_type=MESH,
        )

    def to_right(h, c):
        return lane_copy(me_b - 2 * h, c, me_b + 2, right_send.at[h, c], right_recv.at[h + 1, c])

    def from_left(h, c):
        return lane_copy(me_b - 2 * h, c, me_b, right_send.at[h, c], right_recv.at[h, c])

    def to_left(h, c):
        return lane_copy(me_b + 2 * h, c, me_b - 2, left_send.at[h, c], left_recv.at[h + 1, c])

    def from_right(h, c):
        return lane_copy(me_b + 2 * h, c, me_b, left_send.at[h, c], left_recv.at[h, c])

    def to_pair(origin, c):
        return lane_copy(origin, c, partner, pair_send.at[origin // 2, c], pair_recv.at[origin // 2, c])

    def from_pair(origin_z, c):
        origin = origin_z * 2 + 1 - (me_b % 2)
        return lane_copy(origin, c, partner, pair_send.at[origin_z, c], pair_recv.at[origin_z, c])

    def start_tensor(c, carry):
        own_copy(c).start()
        for step in range(1, tensors):
            tensor_copy(step, c).start()
        return carry

    lax.fori_loop(0, chunks, start_tensor, 0)

    def advance(s, carry):
        @pl.when(s < chunks)
        def _():
            for step in range(1, tensors):
                tensor_copy(step, s).wait_recv()
            own_copy(s).wait()

            @pl.when(has_right)
            def _():
                to_right(0, s).start()

            @pl.when(has_left)
            def _():
                to_left(0, s).start()

            to_pair(me_b, s).start()

        for h in range(1, depth_z):
            c = s - h
            in_range = jnp.logical_and(c >= 0, c < chunks)

            @pl.when(jnp.logical_and(in_range, z - h >= 0))
            def _():
                from_left(h, c).wait_recv()

                @pl.when(has_right)
                def _():
                    to_right(h, c).start()

                to_pair(me_b - 2 * h, c).start()

            @pl.when(jnp.logical_and(in_range, z + h < depth_z))
            def _():
                from_right(h, c).wait_recv()

                @pl.when(has_left)
                def _():
                    to_left(h, c).start()

                to_pair(me_b + 2 * h, c).start()

        return carry

    lax.fori_loop(0, chunks + depth_z - 1, advance, 0)

    def finish(c, carry):
        for step in range(1, tensors):
            tensor_copy(step, c).wait_send()
        for h in range(depth_z):
            from_pair(h, c).wait_recv()
            to_pair(h * 2 + (me_b % 2), c).wait_send()

            @pl.when(jnp.logical_and(has_right, z - h >= 0))
            def _():
                to_right(h, c).wait_send()

            @pl.when(jnp.logical_and(has_left, z + h < depth_z))
            def _():
                to_left(h, c).wait_send()

        return carry

    lax.fori_loop(0, chunks, finish, 0)


def spread(packed, branches, blk_dev, collective):
    tensors, count, rows, width = packed.shape
    depth_z = branches // 2
    chunk = max(1, count // (8 if depth_z <= 4 else 2))
    while count % chunk:
        chunk -= 1
    chunks = count // chunk
    dma = pltpu.SemaphoreType.DMA
    return pl.pallas_call(
        functools.partial(spread_kernel, branches, tensors, count, chunk),
        out_shape=jax.ShapeDtypeStruct((branches, blk_dev, tensors, rows, width), packed.dtype),
        in_specs=[pl.BlockSpec(memory_space=pltpu.VMEM)],
        out_specs=pl.BlockSpec(memory_space=pl.ANY),
        scratch_shapes=[
            dma((tensors - 1, chunks)),
            dma((tensors - 1, chunks)),
            dma((chunks,)),
        ]
        + [dma((depth_z, chunks))] * 6,
        compiler_params=pltpu.CompilerParams(collective_id=collective, has_side_effects=True),
    )(packed)


def relay_kernel(zs, tensors, blk_dev, region, count, first_cols, width, tab_ref, cache_ref, out_ref,
                 stage, landed, pool_x, in_r, in_l, pool_r, pool_l, ring_r, ring_l,
                 x_send, x_recv, x_own, x_psend, x_precv, x_keep,
                 r_send, r_recv, rp_send, rp_recv, r_keep,
                 l_send, l_recv, lp_send, lp_recv, l_keep):
    me_b = lax.axis_index("branch")
    me_t = lax.axis_index("tensor")
    z = me_b // 2
    core = lax.rem(me_b, 2)
    other = 1 - core
    partner = me_b + 1 - 2 * core
    has_left = z > 0
    has_right = z < zs - 1
    group = 2 * K
    pieces = blk_dev // group
    chunks = count // K
    barrier = pltpu.get_barrier_semaphore()
    for step in range(1, tensors):
        pl.semaphore_signal(
            barrier, inc=1, device_id={"tensor": lax.rem(me_t + step, tensors)}, device_id_type=MESH
        )
    pl.semaphore_signal(barrier, inc=1, device_id={"branch": partner}, device_id_type=MESH)

    @pl.when(has_left)
    def _():
        pl.semaphore_signal(barrier, inc=1, device_id={"branch": me_b - 2}, device_id_type=MESH)

    @pl.when(has_right)
    def _():
        pl.semaphore_signal(barrier, inc=1, device_id={"branch": me_b + 2}, device_id_type=MESH)

    pl.semaphore_wait(barrier, tensors + jnp.minimum(z, 1) + jnp.minimum(zs - 1 - z, 1))

    def x_span(x):
        return pl.ds(x * group, group)

    def span(c):
        return pl.ds(c * K, K)

    def share(step, x):
        to = lax.rem(me_t + step, tensors)
        return pltpu.make_async_remote_copy(
            src_ref=stage.at[to, x_span(x)],
            dst_ref=landed.at[x_span(x), me_t],
            send_sem=x_send.at[step - 1, x],
            recv_sem=x_recv.at[step - 1, x],
            device_id={"tensor": to},
            device_id_type=MESH,
        )

    def own_part(x):
        return pltpu.make_async_copy(
            stage.at[me_t, x_span(x)], landed.at[x_span(x), me_t], x_own.at[x]
        )

    def x_pair(x):
        return pltpu.make_async_remote_copy(
            src_ref=landed.at[x_span(x)],
            dst_ref=out_ref.at[x_span(x), core],
            send_sem=x_psend.at[x],
            recv_sem=x_precv.at[x],
            device_id={"branch": partner},
            device_id_type=MESH,
        )

    def x_local(x):
        return pltpu.make_async_copy(landed.at[x_span(x)], out_ref.at[x_span(x), core], x_keep.at[x])

    def send(ring, into, target, send_sem, recv_sem, c):
        return pltpu.make_async_remote_copy(
            src_ref=ring.at[span(lax.rem(c, RING))],
            dst_ref=into.at[span(c), core],
            send_sem=send_sem.at[c],
            recv_sem=recv_sem.at[c],
            device_id={"branch": target},
            device_id_type=MESH,
        )

    def pair(into, send_sem, recv_sem, c):
        return pltpu.make_async_remote_copy(
            src_ref=into.at[span(c), core],
            dst_ref=into.at[span(c), core],
            send_sem=send_sem.at[c],
            recv_sem=recv_sem.at[c],
            device_id={"branch": partner},
            device_id_type=MESH,
        )

    def keep(into, base, lane, keep_sem, c):
        return pltpu.make_async_copy(
            into.at[span(c), lane], out_ref.at[pl.ds(base + c * K, K), lane], keep_sem.at[lane, c]
        )

    flows = (
        (1, ring_r, in_r, pool_r, me_b + 2, has_right, has_left, r_send, r_recv, rp_send, rp_recv,
         r_keep, blk_dev),
        (2, ring_l, in_l, pool_l, me_b - 2, has_left, has_right, l_send, l_recv, lp_send, lp_recv,
         l_keep, blk_dev + region),
    )

    def prepare(x):
        def one(j, carry):
            block = tab_ref[0, x * group + j]
            for t, first in enumerate(first_cols):
                stage[t, x * group + j] = cache_ref[block, :, first : first + width]
            return carry

        lax.fori_loop(0, group, one, 0)
        for step in range(1, tensors):
            share(step, x).start()
        own_part(x).start()

    for x in range(min(2, pieces)):
        prepare(x)

    def advance(s, carry):
        @pl.when(s + 2 < pieces)
        def _():
            prepare(s + 2)

        @pl.when(s < pieces)
        def _():
            for step in range(1, tensors):
                share(step, s).wait_recv()
            own_part(s).wait()
            x_pair(s).start()
            x_local(s).start()

            def one(j, carry):
                pool_x[s * group + j] = landed[s * group + j]
                return carry

            lax.fori_loop(0, group, one, 0)

        for row, ring, into, pool, target, sends, takes, ssem, rsem, pssem, prsem, ksem, base in flows:
            c = s - LAG + 1

            @pl.when(jnp.logical_and(takes, jnp.logical_and(c >= 0, c < chunks)))
            def _():
                send(ring, into, me_b, ssem, rsem, c).wait_recv()
                pair(into, pssem, prsem, c).start()
                keep(into, base, core, ksem, c).start()

        for row, ring, into, pool, target, sends, takes, ssem, rsem, pssem, prsem, ksem, base in flows:
            c = s - LAG

            @pl.when(jnp.logical_and(takes, jnp.logical_and(c >= 0, c < chunks)))
            def _():
                pair(into, pssem, prsem, c).wait_recv()
                keep(into, base, other, ksem, c).start()

                def one(j, carry):
                    pool[2 * (c * K + j)] = into[c * K + j, 0]
                    pool[2 * (c * K + j) + 1] = into[c * K + j, 1]
                    return carry

                lax.fori_loop(0, K, one, 0)

        for row, ring, into, pool, target, sends, takes, ssem, rsem, pssem, prsem, ksem, base in flows:

            @pl.when(jnp.logical_and(sends, s < chunks))
            def _():
                @pl.when(s >= RING)
                def _():
                    send(ring, into, target, ssem, rsem, s - RING).wait_send()

                def one(j, carry):
                    source = tab_ref[row, s * K + j]
                    near = pool_x[jnp.minimum(source, blk_dev - 1)]
                    far = pool[jnp.clip(source - blk_dev, 0, 2 * count - 1)]
                    ring[lax.rem(s, RING) * K + j] = jnp.where(source < blk_dev, near, far)
                    return carry

                lax.fori_loop(0, K, one, 0)
                send(ring, into, target, ssem, rsem, s).start()

        return carry

    lax.fori_loop(0, max(chunks + LAG, pieces), advance, 0)

    def finish_x(x, carry):
        for step in range(1, tensors):
            share(step, x).wait_send()
        x_pair(x).wait()
        x_local(x).wait()
        return carry

    lax.fori_loop(0, pieces, finish_x, 0)

    def finish(c, carry):
        for row, ring, into, pool, target, sends, takes, ssem, rsem, pssem, prsem, ksem, base in flows:

            @pl.when(takes)
            def _():
                pair(into, pssem, prsem, c).wait_send()
                keep(into, base, 0, ksem, c).wait()
                keep(into, base, 1, ksem, c).wait()

            @pl.when(jnp.logical_and(sends, c >= chunks - RING))
            def _():
                send(ring, into, target, ssem, rsem, c).wait_send()

        return carry

    lax.fori_loop(0, chunks, finish, 0)


def relay(table, cache, zs, tensors, count, region, first_cols, width, collective):
    blk_dev, rows, _ = cache.shape
    total = 2 * zs * blk_dev
    dma = pltpu.SemaphoreType.DMA
    pieces = blk_dev // (2 * K)
    chunks = count // K
    block = (tensors, rows, width)
    flow = [dma((chunks,))] * 4 + [dma((2, chunks))]
    return pl.pallas_call(
        functools.partial(
            relay_kernel, zs, tensors, blk_dev, region, count, first_cols, width
        ),
        out_shape=jax.ShapeDtypeStruct((total // 2, 2) + block, cache.dtype),
        in_specs=[pl.BlockSpec(memory_space=pltpu.SMEM), pl.BlockSpec(memory_space=pltpu.VMEM)],
        out_specs=pl.BlockSpec(memory_space=pl.ANY),
        scratch_shapes=[
            pltpu.VMEM((tensors, blk_dev, rows, width), cache.dtype),
            pltpu.VMEM((blk_dev,) + block, cache.dtype),
            pltpu.VMEM((blk_dev,) + block, cache.dtype),
            pltpu.VMEM((count, 2) + block, cache.dtype),
            pltpu.VMEM((count, 2) + block, cache.dtype),
            pltpu.VMEM((2 * count,) + block, cache.dtype),
            pltpu.VMEM((2 * count,) + block, cache.dtype),
            pltpu.VMEM((RING * K,) + block, cache.dtype),
            pltpu.VMEM((RING * K,) + block, cache.dtype),
            dma((tensors - 1, pieces)),
            dma((tensors - 1, pieces)),
        ]
        + [dma((pieces,))] * 4
        + flow
        + flow,
        compiler_params=pltpu.CompilerParams(
            collective_id=collective, has_side_effects=True, vmem_limit_bytes=62 * 2**20
        ),
    )(table, cache)


def attend_kernel(nodes, kv_dev, group_q, tab_ref, q_ref, fresh_ref, *refs):
    kv_refs = refs[:STEP_BLOCKS]
    out_ref, q_s, m_s, l_s, acc_s = refs[STEP_BLOCKS:]
    i = pl.program_id(0)
    factor = math.log2(math.e) / math.sqrt(HD)
    rows = group_q * NODE_TOK
    tile = min(rows, 256)
    contract = (((1,), (1,)), ((), ()))

    @pl.when(i == 0)
    def _():
        row = lax.broadcasted_iota(jnp.int32, (NODE_TOK, NODE_TOK), 0)
        col = lax.broadcasted_iota(jnp.int32, (NODE_TOK, NODE_TOK), 1)
        for n in range(nodes):
            tok = slice(n * NODE_TOK, (n + 1) * NODE_TOK)
            for h in range(kv_dev):
                k = fresh_ref[tok, h * 2 * HD : h * 2 * HD + HD]
                v = fresh_ref[tok, h * 2 * HD + HD : (h + 1) * 2 * HD]
                for a in range(group_q):
                    head = h * group_q + a
                    here = slice(a * NODE_TOK, (a + 1) * NODE_TOK)
                    q = q_ref[tok, head * HD : (head + 1) * HD]
                    q_s[n * kv_dev + h, here, :] = q
                    s = lax.dot_general(q, k, contract, preferred_element_type=jnp.float32)
                    s = jnp.where(col <= row, s * factor, -jnp.inf)
                    m = jnp.max(s, axis=1, keepdims=True)
                    w = jnp.exp2(s - m)
                    m_s[n * kv_dev + h, here, :] = jnp.broadcast_to(m, (NODE_TOK, 128))
                    l_s[n * kv_dev + h, here, :] = w
                    acc_s[n * kv_dev + h, here, :] = jnp.dot(
                        w.astype(jnp.bfloat16), v, preferred_element_type=jnp.float32
                    )

    def visit(n, masked):
        keys = STEP_BLOCKS * BT
        if masked:
            slot = lax.broadcasted_iota(jnp.int32, (1, keys), 1) // BT + i * STEP_BLOCKS
            seen = slot < tab_ref[5, n]
        for h in range(kv_dev):
            k = jnp.concatenate([r[0, :, h * 2 * HD : h * 2 * HD + HD] for r in kv_refs], axis=0)
            v = jnp.concatenate([r[0, :, h * 2 * HD + HD : (h + 1) * 2 * HD] for r in kv_refs], axis=0)
            p = n * kv_dev + h
            for start in range(0, rows, tile):
                here = slice(start, start + tile)
                s = lax.dot_general(
                    q_s[p, here, :], k, contract, preferred_element_type=jnp.float32
                )
                s = s * factor
                if masked:
                    s = jnp.where(seen, s, -jnp.inf)
                m_old = m_s[p, here, :]
                m_new = jnp.maximum(m_old, jnp.max(s, axis=1, keepdims=True))
                alpha = jnp.exp2(m_old - m_new)
                w = [jnp.exp2(s[:, u * 128 : (u + 1) * 128] - m_new) for u in range(keys // 128)]
                l_s[p, here, :] = l_s[p, here, :] * alpha + functools.reduce(jnp.add, w)
                wide = jnp.concatenate([x.astype(jnp.bfloat16) for x in w], axis=1)
                acc_s[p, here, :] = acc_s[p, here, :] * alpha + jnp.dot(
                    wide, v, preferred_element_type=jnp.float32
                )
                m_s[p, here, :] = m_new

    for n in range(nodes):
        first = i * STEP_BLOCKS
        whole = first + STEP_BLOCKS <= tab_ref[5, n]

        @pl.when(whole)
        def _():
            visit(n, False)

        @pl.when(jnp.logical_and(first < tab_ref[5, n], jnp.logical_not(whole)))
        def _():
            visit(n, True)

    @pl.when(i == pl.num_programs(0) - 1)
    def _():
        for n in range(nodes):
            for h in range(kv_dev):
                p = n * kv_dev + h
                for a in range(group_q):
                    head = h * group_q + a
                    here = slice(a * NODE_TOK, (a + 1) * NODE_TOK)
                    total = jnp.sum(l_s[p, here, :], axis=1, keepdims=True)
                    out_ref[n * NODE_TOK : (n + 1) * NODE_TOK, head * HD : (head + 1) * HD] = (
                        acc_s[p, here, :] / total
                    ).astype(out_ref.dtype)


def attend(queries, fresh, blocks, table, nodes, kv_dev, group_q):
    new_rows, q_cols = queries.shape
    width = blocks.shape[2]
    rows = group_q * NODE_TOK
    pairs = nodes * kv_dev

    def kv_spec(u):
        return pl.BlockSpec((1, BT, width), lambda i, tab: (tab[3, i * STEP_BLOCKS + u], 0, 0))

    return pl.pallas_call(
        functools.partial(attend_kernel, nodes, kv_dev, group_q),
        out_shape=jax.ShapeDtypeStruct((new_rows, q_cols), queries.dtype),
        grid_spec=pltpu.PrefetchScalarGridSpec(
            num_scalar_prefetch=1,
            grid=(P_SIZE // STEP_BLOCKS,),
            in_specs=[
                pl.BlockSpec((new_rows, q_cols), lambda i, tab: (0, 0)),
                pl.BlockSpec((new_rows, width), lambda i, tab: (0, 0)),
            ]
            + [kv_spec(u) for u in range(STEP_BLOCKS)],
            out_specs=pl.BlockSpec((new_rows, q_cols), lambda i, tab: (0, 0)),
            scratch_shapes=[
                pltpu.VMEM((pairs, rows, HD), jnp.bfloat16),
                pltpu.VMEM((pairs, rows, 128), jnp.float32),
                pltpu.VMEM((pairs, rows, 128), jnp.float32),
                pltpu.VMEM((pairs, rows, HD), jnp.float32),
            ],
        ),
        compiler_params=pltpu.CompilerParams(vmem_limit_bytes=48 * 2**20),
    )(table, queries, fresh, *([blocks] * STEP_BLOCKS))


def body(queries, new_kv, cache, parents, depth):
    tensor_size = lax.axis_size("tensor")
    branches = lax.axis_size("branch")
    tensor_pos = lax.axis_index("tensor")
    branch_pos = lax.axis_index("branch")
    sharing = HQ // KVH
    heads_dev = queries.shape[1] // HD
    kv_dev = max(1, heads_dev // sharing)
    group_q = heads_dev // kv_dev
    first_kv = tensor_pos * heads_dev // sharing
    blk_dev = cache.shape[0]
    new_rows = queries.shape[0]
    width = kv_dev * 2 * HD
    nodes = depth.shape[1]
    zs = branches // 2
    first_cols = [(t * heads_dev // sharing) * 2 * HD for t in range(tensor_size)]
    fresh = lax.dynamic_slice_in_dim(new_kv, first_kv, kv_dev, 1).reshape(new_rows, width)
    out_blocks = (branches * blk_dev // 2, 2, tensor_size, cache.shape[1], width)

    def flood(cache, picks, collective):
        packed = pack(cache, picks, blk_dev, first_cols, width)
        return spread(packed, branches, blk_dev, collective).reshape(out_blocks)

    region = (branches * blk_dev - 2 * blk_dev) // 4
    every = jnp.arange(blk_dev, dtype=jnp.int32)
    if zs <= 4 and blk_dev % (2 * K) == 0 and region >= LEVELS[-1] and branches * blk_dev <= 256:
        table = make_plan(parents, depth, branches, blk_dev, region)

        def with_count(count, collective):
            def run(table, cache):
                return relay(
                    table, cache, zs, tensor_size, count, region, first_cols, width, collective
                )

            return run

        runs = [with_count(count, 1 + i) for i, count in enumerate(LEVELS)]
        runs.append(lambda table, cache: flood(cache, every, 1 + len(LEVELS)))
        gathered = lax.switch(table[4, 0], runs, table, cache)
    else:
        own_row = lax.dynamic_index_in_dim(parents, branch_pos, 0, keepdims=False)
        own_row = own_row[jnp.minimum(jnp.arange(P_SIZE), jnp.max(depth[0]) - 1)]
        filler = jnp.zeros((128,), jnp.int32)
        rows = [filler] * 3 + [filler.at[:P_SIZE].set(own_row), filler, filler.at[:nodes].set(depth[0])]
        table = jnp.stack(rows + [filler] * 2)
        gathered = flood(cache, every, 1)
    blocks = gathered.reshape(branches * blk_dev, BT, width)
    return attend(queries, fresh, blocks, table, nodes, kv_dev, group_q)


def solution(mesh):
    placed = (
        P("branch", "tensor"),
        P("branch", None, None),
        P("branch", "tensor", None),
        P(),
        P("branch", None),
    )
    return jax.shard_map(
        body, mesh=mesh, in_specs=placed, out_specs=P("branch", "tensor"), check_vma=False
    )
```

```python
import functools
import math

import jax
import jax.numpy as jnp
from jax import lax
from jax.experimental import pallas as pl
from jax.experimental.pallas import tpu as pltpu
from jax.sharding import PartitionSpec as P

HQ = 64
KVH = 8
HD = 128
BT = 128
NODE_TOK = 128
P_SIZE = 48
STEP_BLOCKS = 4
K = 2
LAG = 3
RING = 4
LEVELS = (24, 26, 28, 30, 34, 42)
MESH = pl.DeviceIdType.MESH


def plan(zs, blk_dev, region, levels, parents, deep, me):
    n = 2 * zs
    nb = n * blk_dev
    big = 1 << 20
    i32 = jnp.int32
    lane = lax.broadcasted_iota(i32, (n, 128), 1)
    act = jnp.where(lane < deep, parents, -1)
    blk = lax.broadcasted_iota(i32, (nb, 128), 0)
    need = []
    for z in range(zs):
        hit = (act[2 * z : 2 * z + 1, :] == blk) | (act[2 * z + 1 : 2 * z + 2, :] == blk)
        need.append(jnp.max(jnp.where(hit, 1, 0), axis=1, keepdims=True) > 0)
    bcol = lax.broadcasted_iota(i32, (nb, 1), 0)
    owner = jnp.zeros((nb, 1), i32)
    for o in range(1, n):
        owner = owner + jnp.where(bcol >= o * blk_dev, 1, 0)
    zb = owner >> 1
    cb = owner & 1
    eye = lax.broadcasted_iota(i32, (nb, nb), 0) == lax.broadcasted_iota(i32, (nb, nb), 1)

    def row(x):
        return jnp.sum(jnp.where(eye, x, 0), axis=0, keepdims=True)

    def rank(key):
        return jnp.sum(jnp.where(row(key) < key, 1, 0), axis=1, keepdims=True)

    def direction(fwd):
        zc = zb if fwd else zs - 1 - zb
        far = jnp.full((nb, 1), -1, i32)
        for z in range(zs):
            zz = z if fwd else zs - 1 - z
            far = jnp.where(need[z] & (zz > zc), jnp.maximum(far, zz), far)
        own_rank = jnp.full((nb, 1), big, i32)
        slots = []
        total = jnp.zeros((1, 1), i32)
        prev = jnp.zeros((nb, 1), i32)
        for k in range(zs - 1):
            own = (zc == k) & (far > k)
            rel = (zc < k) & (far > k)
            first = (cb * zs + (zs - far)) * nb + bcol
            key = jnp.where(own, first, jnp.where(rel, big + prev, 2 * big + bcol))
            key_row = row(key)
            r0 = jnp.sum(jnp.where(key_row < key, 1, 0), axis=1, keepdims=True)
            n0 = jnp.sum(jnp.where(own & (cb == 0), 1, 0), axis=0, keepdims=True)
            n1 = jnp.sum(jnp.where(own & (cb == 1), 1, 0), axis=0, keepdims=True)
            top = jnp.maximum(n0, n1)
            short = jnp.where(n0 <= n1, 0, 1)
            mine = r0 - cb * n0
            if k > 0:
                ready = (prev >> (K.bit_length())) + LAG
                at = jnp.where(ready * K <= top, top + ready * K, 2 * K * ready)
                gap_row = row(jnp.where(rel, at - r0, -big))
                gap = jnp.max(jnp.where(key_row <= key, gap_row, -big), axis=1, keepdims=True)
                r = r0 + jnp.maximum(gap, 0)
            else:
                r = r0
            far_slot = jnp.where(r < 2 * top, 2 * (r - top) + short, r)
            q = jnp.where(own, 2 * mine + cb, jnp.where(rel, far_slot, -1))
            own_rank = jnp.where(own, mine, own_rank)
            total = jnp.maximum(total, jnp.max(q, axis=0, keepdims=True) + 1)
            slots.append(q)
            prev = jnp.maximum(q, 0)
        return slots, own_rank, total

    right, rank_r, total_r = direction(True)
    left, rank_l, total_l = direction(False)
    local = jnp.zeros((nb, 1), jnp.bool_)
    for z in range(zs):
        local = local | (need[z] & (zb == z))
    key = jnp.minimum(2 * rank_r, 2 * rank_l + 1)
    key = jnp.where(key < big, key, jnp.where(local, big // 2 + bcol, big + bcol))
    order = rank(owner * (4 * big) + key) - owner * blk_dev

    me_z = me // 2
    me_c = me % 2
    lanes = lax.broadcasted_iota(i32, (1, 128), 1)

    def table(where_col, value_col):
        return jnp.sum(jnp.where(where_col == lanes, value_col, 0), axis=0, keepdims=True)

    def pick_link(slots, k):
        q = jnp.full((nb, 1), -1, i32)
        for j in range(zs - 1):
            q = jnp.where(k == j, slots[j], q)
        return q

    mine = owner == me
    picks = table(jnp.where(mine, order, -1), bcol - owner * blk_dev)

    def sources(slots, k):
        q = pick_link(slots, k)
        came = pick_link(slots, k - 1)
        source = jnp.where(zb == me_z, order, blk_dev + came)
        use = (q >= 0) & ((q & 1) == me_c)
        return table(jnp.where(use, q >> 1, -1), source)

    sel_r = sources(right, me_z)
    sel_l = sources(left, zs - 1 - me_z)
    from_r = pick_link(right, me_z - 1)
    from_l = pick_link(left, zs - 2 - me_z)
    place = jnp.where(
        zb == me_z,
        2 * order + cb,
        jnp.where(zb < me_z, 2 * blk_dev + from_r, 2 * (blk_dev + region) + from_l),
    )
    slot_count = (jnp.maximum(total_r, total_l) + 1) >> 1
    choice = jnp.zeros((1, 1), i32)
    for c in levels:
        choice = choice + jnp.where(slot_count > c, 1, 0)
    place = jnp.where(choice == len(levels), bcol, place)
    groups = lax.broadcasted_iota(i32, (n, 128), 0)
    my_row = jnp.sum(jnp.where(groups == me, act, 0), axis=0, keepdims=True)
    last = jnp.sum(jnp.where((groups == me) & (lane == deep - 1), act, 0), axis=(0, 1), keepdims=True)
    my_row = jnp.where(my_row < 0, last, my_row)
    pos = jnp.sum(jnp.where(bcol == my_row, place, 0), axis=0, keepdims=True)
    return picks, sel_r, sel_l, pos, choice, slot_count


def plan_kernel(zs, blk_dev, region, parents_ref, mine_ref, table_ref, all_ref, send_sem, recv_sem):
    n = 2 * zs
    me = lax.axis_index("branch")
    barrier = pltpu.get_barrier_semaphore()

    def greet(i, carry):
        peer = lax.rem(me + i, n)
        pl.semaphore_signal(barrier, inc=1, device_id={"branch": peer}, device_id_type=MESH)
        return carry

    lax.fori_loop(1, n, greet, 0)
    pl.semaphore_wait(barrier, n - 1)

    def copy(i):
        return pltpu.make_async_remote_copy(
            src_ref=mine_ref,
            dst_ref=all_ref.at[me],
            send_sem=send_sem.at[i],
            recv_sem=recv_sem.at[i],
            device_id={"branch": lax.rem(me + i, n)},
            device_id_type=MESH,
        )

    def start(i, carry):
        copy(i).start()
        return carry

    def finish(i, carry):
        copy(i).wait()
        return carry

    lax.fori_loop(1, n, start, 0)
    all_ref[pl.ds(me, 1)] = mine_ref[...][None]
    lax.fori_loop(1, n, finish, 0)
    deep = jnp.concatenate([jnp.max(all_ref[g, 0:1, :], axis=1, keepdims=True) for g in range(n)], axis=0)
    picks, sel_r, sel_l, pos, choice, _ = plan(
        zs, blk_dev, region, LEVELS, parents_ref[...], deep, me
    )
    wide = jnp.broadcast_to(choice, (1, 128))
    table_ref[...] = jnp.concatenate(
        [picks, sel_r, sel_l, pos, wide, mine_ref[0:1, :], wide, wide], axis=0
    )


def make_plan(parents, depth, n, blk_dev, region):
    nodes = depth.shape[1]
    mine = jnp.zeros((8, 128), jnp.int32) + jnp.pad(depth, ((0, 0), (0, 128 - nodes)))
    listed = jnp.pad(parents, ((0, 0), (0, 128 - parents.shape[1])), constant_values=-1)
    return pl.pallas_call(
        functools.partial(plan_kernel, n // 2, blk_dev, region),
        out_shape=jax.ShapeDtypeStruct((8, 128), jnp.int32),
        in_specs=[pl.BlockSpec(memory_space=pltpu.VMEM)] * 2,
        out_specs=pl.BlockSpec(memory_space=pltpu.VMEM),
        scratch_shapes=[
            pltpu.VMEM((n, 8, 128), jnp.int32),
            pltpu.SemaphoreType.DMA((n,)),
            pltpu.SemaphoreType.DMA((n,)),
        ],
        compiler_params=pltpu.CompilerParams(collective_id=0, has_side_effects=True),
    )(listed, mine)


def pack_kernel(first_cols, width, pick_ref, block_ref, packed_ref):
    for t, first in enumerate(first_cols):
        packed_ref[t, 0] = block_ref[0, :, first : first + width]


def pack(cache, picks, count, first_cols, width):
    rows = cache.shape[1]
    tensors = len(first_cols)
    return pl.pallas_call(
        functools.partial(pack_kernel, first_cols, width),
        out_shape=jax.ShapeDtypeStruct((tensors, count, rows, width), cache.dtype),
        grid_spec=pltpu.PrefetchScalarGridSpec(
            num_scalar_prefetch=1,
            grid=(count,),
            in_specs=[pl.BlockSpec((1, rows, cache.shape[2]), lambda i, pick: (pick[i], 0, 0))],
            out_specs=pl.BlockSpec((tensors, 1, rows, width), lambda i, pick: (0, i, 0, 0)),
        ),
    )(picks, cache)


def spread_kernel(branches, tensors, count, chunk, packed_ref, out_ref, tp_send, tp_recv, own_sem,
                  right_send, right_recv, left_send, left_recv, pair_send, pair_recv):
    me_b = lax.axis_index("branch")
    me_t = lax.axis_index("tensor")
    z = me_b // 2
    depth_z = branches // 2
    partner = me_b + 1 - 2 * (me_b % 2)
    chunks = count // chunk
    has_left = z > 0
    has_right = z < depth_z - 1
    barrier = pltpu.get_barrier_semaphore()
    for step in range(1, tensors):
        pl.semaphore_signal(
            barrier, inc=1, device_id={"tensor": lax.rem(me_t + step, tensors)}, device_id_type=MESH
        )
    pl.semaphore_signal(barrier, inc=1, device_id={"branch": partner}, device_id_type=MESH)

    @pl.when(has_left)
    def _():
        pl.semaphore_signal(barrier, inc=1, device_id={"branch": me_b - 2}, device_id_type=MESH)

    @pl.when(has_right)
    def _():
        pl.semaphore_signal(barrier, inc=1, device_id={"branch": me_b + 2}, device_id_type=MESH)

    pl.semaphore_wait(barrier, tensors + jnp.minimum(z, 1) + jnp.minimum(depth_z - 1 - z, 1))

    def span(c):
        return pl.ds(c * chunk, chunk)

    def tensor_copy(step, c):
        to = lax.rem(me_t + step, tensors)
        return pltpu.make_async_remote_copy(
            src_ref=packed_ref.at[to, span(c)],
            dst_ref=out_ref.at[me_b, span(c), me_t],
            send_sem=tp_send.at[step - 1, c],
            recv_sem=tp_recv.at[step - 1, c],
            device_id={"tensor": to},
            device_id_type=MESH,
        )

    def own_copy(c):
        return pltpu.make_async_copy(
            packed_ref.at[me_t, span(c)], out_ref.at[me_b, span(c), me_t], own_sem.at[c]
        )

    def lane_copy(origin, c, target, send_sem, recv_sem):
        return pltpu.make_async_remote_copy(
            src_ref=out_ref.at[origin, span(c)],
            dst_ref=out_ref.at[origin, span(c)],
            send_sem=send_sem,
            recv_sem=recv_sem,
            device_id={"branch": target},
            device_id_type=MESH,
        )

    def to_right(h, c):
        return lane_copy(me_b - 2 * h, c, me_b + 2, right_send.at[h, c], right_recv.at[h + 1, c])

    def from_left(h, c):
        return lane_copy(me_b - 2 * h, c, me_b, right_send.at[h, c], right_recv.at[h, c])

    def to_left(h, c):
        return lane_copy(me_b + 2 * h, c, me_b - 2, left_send.at[h, c], left_recv.at[h + 1, c])

    def from_right(h, c):
        return lane_copy(me_b + 2 * h, c, me_b, left_send.at[h, c], left_recv.at[h, c])

    def to_pair(origin, c):
        return lane_copy(origin, c, partner, pair_send.at[origin // 2, c], pair_recv.at[origin // 2, c])

    def from_pair(origin_z, c):
        origin = origin_z * 2 + 1 - (me_b % 2)
        return lane_copy(origin, c, partner, pair_send.at[origin_z, c], pair_recv.at[origin_z, c])

    def start_tensor(c, carry):
        own_copy(c).start()
        for step in range(1, tensors):
            tensor_copy(step, c).start()
        return carry

    lax.fori_loop(0, chunks, start_tensor, 0)

    def advance(s, carry):
        @pl.when(s < chunks)
        def _():
            for step in range(1, tensors):
                tensor_copy(step, s).wait_recv()
            own_copy(s).wait()

            @pl.when(has_right)
            def _():
                to_right(0, s).start()

            @pl.when(has_left)
            def _():
                to_left(0, s).start()

            to_pair(me_b, s).start()

        for h in range(1, depth_z):
            c = s - h
            in_range = jnp.logical_and(c >= 0, c < chunks)

            @pl.when(jnp.logical_and(in_range, z - h >= 0))
            def _():
                from_left(h, c).wait_recv()

                @pl.when(has_right)
                def _():
                    to_right(h, c).start()

                to_pair(me_b - 2 * h, c).start()

            @pl.when(jnp.logical_and(in_range, z + h < depth_z))
            def _():
                from_right(h, c).wait_recv()

                @pl.when(has_left)
                def _():
                    to_left(h, c).start()

                to_pair(me_b + 2 * h, c).start()

        return carry

    lax.fori_loop(0, chunks + depth_z - 1, advance, 0)

    def finish(c, carry):
        for step in range(1, tensors):
            tensor_copy(step, c).wait_send()
        for h in range(depth_z):
            from_pair(h, c).wait_recv()
            to_pair(h * 2 + (me_b % 2), c).wait_send()

            @pl.when(jnp.logical_and(has_right, z - h >= 0))
            def _():
                to_right(h, c).wait_send()

            @pl.when(jnp.logical_and(has_left, z + h < depth_z))
            def _():
                to_left(h, c).wait_send()

        return carry

    lax.fori_loop(0, chunks, finish, 0)


def spread(packed, branches, blk_dev, collective):
    tensors, count, rows, width = packed.shape
    depth_z = branches // 2
    chunk = max(1, count // (8 if depth_z <= 4 else 2))
    while count % chunk:
        chunk -= 1
    chunks = count // chunk
    dma = pltpu.SemaphoreType.DMA
    return pl.pallas_call(
        functools.partial(spread_kernel, branches, tensors, count, chunk),
        out_shape=jax.ShapeDtypeStruct((branches, blk_dev, tensors, rows, width), packed.dtype),
        in_specs=[pl.BlockSpec(memory_space=pltpu.VMEM)],
        out_specs=pl.BlockSpec(memory_space=pl.ANY),
        scratch_shapes=[
            dma((tensors - 1, chunks)),
            dma((tensors - 1, chunks)),
            dma((chunks,)),
        ]
        + [dma((depth_z, chunks))] * 6,
        compiler_params=pltpu.CompilerParams(collective_id=collective, has_side_effects=True),
    )(packed)


def relay_kernel(zs, tensors, blk_dev, region, count, first_cols, width, tab_ref, cache_ref, out_ref,
                 stage, landed, pool_x, in_r, in_l, pool_r, pool_l, ring_r, ring_l,
                 x_send, x_recv, x_own, x_psend, x_precv, x_keep,
                 r_send, r_recv, rp_send, rp_recv, r_keep,
                 l_send, l_recv, lp_send, lp_recv, l_keep):
    me_b = lax.axis_index("branch")
    me_t = lax.axis_index("tensor")
    z = me_b // 2
    core = lax.rem(me_b, 2)
    other = 1 - core
    partner = me_b + 1 - 2 * core
    has_left = z > 0
    has_right = z < zs - 1
    group = 2 * K
    pieces = blk_dev // group
    chunks = count // K
    barrier = pltpu.get_barrier_semaphore()
    for step in range(1, tensors):
        pl.semaphore_signal(
            barrier, inc=1, device_id={"tensor": lax.rem(me_t + step, tensors)}, device_id_type=MESH
        )
    pl.semaphore_signal(barrier, inc=1, device_id={"branch": partner}, device_id_type=MESH)

    @pl.when(has_left)
    def _():
        pl.semaphore_signal(barrier, inc=1, device_id={"branch": me_b - 2}, device_id_type=MESH)

    @pl.when(has_right)
    def _():
        pl.semaphore_signal(barrier, inc=1, device_id={"branch": me_b + 2}, device_id_type=MESH)

    pl.semaphore_wait(barrier, tensors + jnp.minimum(z, 1) + jnp.minimum(zs - 1 - z, 1))

    def x_span(x):
        return pl.ds(x * group, group)

    def span(c):
        return pl.ds(c * K, K)

    def share(step, x):
        to = lax.rem(me_t + step, tensors)
        return pltpu.make_async_remote_copy(
            src_ref=stage.at[to, x_span(x)],
            dst_ref=landed.at[x_span(x), me_t],
            send_sem=x_send.at[step - 1, x],
            recv_sem=x_recv.at[step - 1, x],
            device_id={"tensor": to},
            device_id_type=MESH,
        )

    def own_part(x):
        return pltpu.make_async_copy(
            stage.at[me_t, x_span(x)], landed.at[x_span(x), me_t], x_own.at[x]
        )

    def x_pair(x):
        return pltpu.make_async_remote_copy(
            src_ref=landed.at[x_span(x)],
            dst_ref=out_ref.at[x_span(x), core],
            send_sem=x_psend.at[x],
            recv_sem=x_precv.at[x],
            device_id={"branch": partner},
            device_id_type=MESH,
        )

    def x_local(x):
        return pltpu.make_async_copy(landed.at[x_span(x)], out_ref.at[x_span(x), core], x_keep.at[x])

    def send(ring, into, target, send_sem, recv_sem, c):
        return pltpu.make_async_remote_copy(
            src_ref=ring.at[span(lax.rem(c, RING))],
            dst_ref=into.at[span(c), core],
            send_sem=send_sem.at[c],
            recv_sem=recv_sem.at[c],
            device_id={"branch": target},
            device_id_type=MESH,
        )

    def pair(into, send_sem, recv_sem, c):
        return pltpu.make_async_remote_copy(
            src_ref=into.at[span(c), core],
            dst_ref=into.at[span(c), core],
            send_sem=send_sem.at[c],
            recv_sem=recv_sem.at[c],
            device_id={"branch": partner},
            device_id_type=MESH,
        )

    def keep(into, base, lane, keep_sem, c):
        return pltpu.make_async_copy(
            into.at[span(c), lane], out_ref.at[pl.ds(base + c * K, K), lane], keep_sem.at[lane, c]
        )

    flows = (
        (1, ring_r, in_r, pool_r, me_b + 2, has_right, has_left, r_send, r_recv, rp_send, rp_recv,
         r_keep, blk_dev),
        (2, ring_l, in_l, pool_l, me_b - 2, has_left, has_right, l_send, l_recv, lp_send, lp_recv,
         l_keep, blk_dev + region),
    )

    def prepare(x):
        def one(j, carry):
            block = tab_ref[0, x * group + j]
            for t, first in enumerate(first_cols):
                stage[t, x * group + j] = cache_ref[block, :, first : first + width]
            return carry

        lax.fori_loop(0, group, one, 0)
        for step in range(1, tensors):
            share(step, x).start()
        own_part(x).start()

    for x in range(min(2, pieces)):
        prepare(x)

    def advance(s, carry):
        @pl.when(s + 2 < pieces)
        def _():
            prepare(s + 2)

        @pl.when(s < pieces)
        def _():
            for step in range(1, tensors):
                share(step, s).wait_recv()
            own_part(s).wait()
            x_pair(s).start()
            x_local(s).start()

            def one(j, carry):
                pool_x[s * group + j] = landed[s * group + j]
                return carry

            lax.fori_loop(0, group, one, 0)

        for row, ring, into, pool, target, sends, takes, ssem, rsem, pssem, prsem, ksem, base in flows:
            c = s - LAG + 1

            @pl.when(jnp.logical_and(takes, jnp.logical_and(c >= 0, c < chunks)))
            def _():
                send(ring, into, me_b, ssem, rsem, c).wait_recv()
                pair(into, pssem, prsem, c).start()
                keep(into, base, core, ksem, c).start()

        for row, ring, into, pool, target, sends, takes, ssem, rsem, pssem, prsem, ksem, base in flows:
            c = s - LAG

            @pl.when(jnp.logical_and(takes, jnp.logical_and(c >= 0, c < chunks)))
            def _():
                pair(into, pssem, prsem, c).wait_recv()
                keep(into, base, other, ksem, c).start()

                def one(j, carry):
                    pool[2 * (c * K + j)] = into[c * K + j, 0]
                    pool[2 * (c * K + j) + 1] = into[c * K + j, 1]
                    return carry

                lax.fori_loop(0, K, one, 0)

        for row, ring, into, pool, target, sends, takes, ssem, rsem, pssem, prsem, ksem, base in flows:

            @pl.when(jnp.logical_and(sends, s < chunks))
            def _():
                @pl.when(s >= RING)
                def _():
                    send(ring, into, target, ssem, rsem, s - RING).wait_send()

                def one(j, carry):
                    source = tab_ref[row, s * K + j]
                    near = pool_x[jnp.minimum(source, blk_dev - 1)]
                    far = pool[jnp.clip(source - blk_dev, 0, 2 * count - 1)]
                    ring[lax.rem(s, RING) * K + j] = jnp.where(source < blk_dev, near, far)
                    return carry

                lax.fori_loop(0, K, one, 0)
                send(ring, into, target, ssem, rsem, s).start()

        return carry

    lax.fori_loop(0, max(chunks + LAG, pieces), advance, 0)

    def finish_x(x, carry):
        for step in range(1, tensors):
            share(step, x).wait_send()
        x_pair(x).wait()
        x_local(x).wait()
        return carry

    lax.fori_loop(0, pieces, finish_x, 0)

    def finish(c, carry):
        for row, ring, into, pool, target, sends, takes, ssem, rsem, pssem, prsem, ksem, base in flows:

            @pl.when(takes)
            def _():
                pair(into, pssem, prsem, c).wait_send()
                keep(into, base, 0, ksem, c).wait()
                keep(into, base, 1, ksem, c).wait()

            @pl.when(jnp.logical_and(sends, c >= chunks - RING))
            def _():
                send(ring, into, target, ssem, rsem, c).wait_send()

        return carry

    lax.fori_loop(0, chunks, finish, 0)


def relay(table, cache, zs, tensors, count, region, first_cols, width, collective):
    blk_dev, rows, _ = cache.shape
    total = 2 * zs * blk_dev
    dma = pltpu.SemaphoreType.DMA
    pieces = blk_dev // (2 * K)
    chunks = count // K
    block = (tensors, rows, width)
    flow = [dma((chunks,))] * 4 + [dma((2, chunks))]
    return pl.pallas_call(
        functools.partial(
            relay_kernel, zs, tensors, blk_dev, region, count, first_cols, width
        ),
        out_shape=jax.ShapeDtypeStruct((total // 2, 2) + block, cache.dtype),
        in_specs=[pl.BlockSpec(memory_space=pltpu.SMEM), pl.BlockSpec(memory_space=pltpu.VMEM)],
        out_specs=pl.BlockSpec(memory_space=pl.ANY),
        scratch_shapes=[
            pltpu.VMEM((tensors, blk_dev, rows, width), cache.dtype),
            pltpu.VMEM((blk_dev,) + block, cache.dtype),
            pltpu.VMEM((blk_dev,) + block, cache.dtype),
            pltpu.VMEM((count, 2) + block, cache.dtype),
            pltpu.VMEM((count, 2) + block, cache.dtype),
            pltpu.VMEM((2 * count,) + block, cache.dtype),
            pltpu.VMEM((2 * count,) + block, cache.dtype),
            pltpu.VMEM((RING * K,) + block, cache.dtype),
            pltpu.VMEM((RING * K,) + block, cache.dtype),
            dma((tensors - 1, pieces)),
            dma((tensors - 1, pieces)),
        ]
        + [dma((pieces,))] * 4
        + flow
        + flow,
        compiler_params=pltpu.CompilerParams(
            collective_id=collective, has_side_effects=True, vmem_limit_bytes=62 * 2**20
        ),
    )(table, cache)


def attend_kernel(nodes, kv_dev, group_q, tab_ref, q_ref, fresh_ref, *refs):
    kv_refs = refs[:STEP_BLOCKS]
    out_ref, q_s, m_s, l_s, acc_s = refs[STEP_BLOCKS:]
    i = pl.program_id(0)
    factor = math.log2(math.e) / math.sqrt(HD)
    rows = group_q * NODE_TOK
    tile = min(rows, 256)
    contract = (((1,), (1,)), ((), ()))

    @pl.when(i == 0)
    def _():
        row = lax.broadcasted_iota(jnp.int32, (NODE_TOK, NODE_TOK), 0)
        col = lax.broadcasted_iota(jnp.int32, (NODE_TOK, NODE_TOK), 1)
        for n in range(nodes):
            tok = slice(n * NODE_TOK, (n + 1) * NODE_TOK)
            for h in range(kv_dev):
                k = fresh_ref[tok, h * 2 * HD : h * 2 * HD + HD]
                v = fresh_ref[tok, h * 2 * HD + HD : (h + 1) * 2 * HD]
                for a in range(group_q):
                    head = h * group_q + a
                    here = slice(a * NODE_TOK, (a + 1) * NODE_TOK)
                    q = q_ref[tok, head * HD : (head + 1) * HD]
                    wide_q = q.astype(jnp.float32) * factor
                    upper = wide_q.astype(jnp.bfloat16)
                    q_s[n * kv_dev + h, here, :HD] = upper
                    q_s[n * kv_dev + h, here, HD:] = (wide_q - upper.astype(jnp.float32)).astype(jnp.bfloat16)
                    s = lax.dot_general(q, k, contract, preferred_element_type=jnp.float32)
                    s = jnp.where(col <= row, s * factor, -jnp.inf)
                    m = jnp.max(s, axis=1, keepdims=True)
                    w = jnp.exp2(s - m)
                    m_s[n * kv_dev + h, here, :] = jnp.broadcast_to(m, (NODE_TOK, 128))
                    l_s[n * kv_dev + h, here, :] = jnp.broadcast_to(jnp.sum(w, axis=1, keepdims=True), (NODE_TOK, 128))
                    acc_s[n * kv_dev + h, here, :] = jnp.dot(
                        w.astype(jnp.bfloat16), v, preferred_element_type=jnp.float32
                    )

    def visit(n, masked):
        keys = STEP_BLOCKS * BT
        if masked:
            slot = lax.broadcasted_iota(jnp.int32, (1, keys), 1) // BT + i * STEP_BLOCKS
            seen = slot < tab_ref[5, n]
        for h in range(kv_dev):
            k = jnp.concatenate([r[0, :, h * 2 * HD : h * 2 * HD + HD] for r in kv_refs], axis=0)
            v = jnp.concatenate([r[0, :, h * 2 * HD + HD : (h + 1) * 2 * HD] for r in kv_refs], axis=0)
            vv = jnp.concatenate([v, jnp.ones_like(v)], axis=1)
            kk = jnp.concatenate([k, k], axis=1)
            p = n * kv_dev + h
            for start in range(0, rows, tile):
                here = slice(start, start + tile)
                s = lax.dot_general(
                    q_s[p, here, :], kk, contract, preferred_element_type=jnp.float32
                )
                if masked:
                    s = jnp.where(seen, s, -jnp.inf)
                m_old = m_s[p, here, :]
                m_new = jnp.maximum(m_old, jnp.max(s, axis=1, keepdims=True))
                alpha = jnp.exp2(m_old - m_new)
                w = [jnp.exp2(s[:, u * 128 : (u + 1) * 128] - m_new) for u in range(keys // 128)]
                wide = jnp.concatenate([x.astype(jnp.bfloat16) for x in w], axis=1)
                both = jnp.dot(wide, vv, preferred_element_type=jnp.float32)
                acc_s[p, here, :] = acc_s[p, here, :] * alpha + both[:, :HD]
                l_s[p, here, :] = l_s[p, here, :] * alpha + both[:, HD:]
                m_s[p, here, :] = m_new

    for n in range(nodes):
        first = i * STEP_BLOCKS
        whole = first + STEP_BLOCKS <= tab_ref[5, n]

        @pl.when(whole)
        def _():
            visit(n, False)

        @pl.when(jnp.logical_and(first < tab_ref[5, n], jnp.logical_not(whole)))
        def _():
            visit(n, True)

    @pl.when(i == pl.num_programs(0) - 1)
    def _():
        for n in range(nodes):
            for h in range(kv_dev):
                p = n * kv_dev + h
                for a in range(group_q):
                    head = h * group_q + a
                    here = slice(a * NODE_TOK, (a + 1) * NODE_TOK)
                    total = l_s[p, here, :]
                    out_ref[n * NODE_TOK : (n + 1) * NODE_TOK, head * HD : (head + 1) * HD] = (
                        acc_s[p, here, :] / total
                    ).astype(out_ref.dtype)


def attend(queries, fresh, blocks, table, nodes, kv_dev, group_q):
    new_rows, q_cols = queries.shape
    width = blocks.shape[2]
    rows = group_q * NODE_TOK
    pairs = nodes * kv_dev

    def kv_spec(u):
        return pl.BlockSpec((1, BT, width), lambda i, tab: (tab[3, i * STEP_BLOCKS + u], 0, 0))

    return pl.pallas_call(
        functools.partial(attend_kernel, nodes, kv_dev, group_q),
        out_shape=jax.ShapeDtypeStruct((new_rows, q_cols), queries.dtype),
        grid_spec=pltpu.PrefetchScalarGridSpec(
            num_scalar_prefetch=1,
            grid=(P_SIZE // STEP_BLOCKS,),
            in_specs=[
                pl.BlockSpec((new_rows, q_cols), lambda i, tab: (0, 0)),
                pl.BlockSpec((new_rows, width), lambda i, tab: (0, 0)),
            ]
            + [kv_spec(u) for u in range(STEP_BLOCKS)],
            out_specs=pl.BlockSpec((new_rows, q_cols), lambda i, tab: (0, 0)),
            scratch_shapes=[
                pltpu.VMEM((pairs, rows, 2 * HD), jnp.bfloat16),
                pltpu.VMEM((pairs, rows, 128), jnp.float32),
                pltpu.VMEM((pairs, rows, 128), jnp.float32),
                pltpu.VMEM((pairs, rows, HD), jnp.float32),
            ],
        ),
        compiler_params=pltpu.CompilerParams(vmem_limit_bytes=48 * 2**20),
    )(table, queries, fresh, *([blocks] * STEP_BLOCKS))


def body(queries, new_kv, cache, parents, depth):
    tensor_size = lax.axis_size("tensor")
    branches = lax.axis_size("branch")
    tensor_pos = lax.axis_index("tensor")
    branch_pos = lax.axis_index("branch")
    sharing = HQ // KVH
    heads_dev = queries.shape[1] // HD
    kv_dev = max(1, heads_dev // sharing)
    group_q = heads_dev // kv_dev
    first_kv = tensor_pos * heads_dev // sharing
    blk_dev = cache.shape[0]
    new_rows = queries.shape[0]
    width = kv_dev * 2 * HD
    nodes = depth.shape[1]
    zs = branches // 2
    first_cols = [(t * heads_dev // sharing) * 2 * HD for t in range(tensor_size)]
    fresh = lax.dynamic_slice_in_dim(new_kv, first_kv, kv_dev, 1).reshape(new_rows, width)
    out_blocks = (branches * blk_dev // 2, 2, tensor_size, cache.shape[1], width)

    def flood(cache, picks, collective):
        packed = pack(cache, picks, blk_dev, first_cols, width)
        return spread(packed, branches, blk_dev, collective).reshape(out_blocks)

    region = (branches * blk_dev - 2 * blk_dev) // 4
    every = jnp.arange(blk_dev, dtype=jnp.int32)
    if zs <= 4 and blk_dev % (2 * K) == 0 and region >= LEVELS[-1] and branches * blk_dev <= 256:
        table = make_plan(parents, depth, branches, blk_dev, region)

        def with_count(count, collective):
            def run(table, cache):
                return relay(
                    table, cache, zs, tensor_size, count, region, first_cols, width, collective
                )

            return run

        runs = [with_count(count, 1 + i) for i, count in enumerate(LEVELS)]
        runs.append(lambda table, cache: flood(cache, every, 1 + len(LEVELS)))
        gathered = lax.switch(table[4, 0], runs, table, cache)
    else:
        own_row = lax.dynamic_index_in_dim(parents, branch_pos, 0, keepdims=False)
        own_row = own_row[jnp.minimum(jnp.arange(P_SIZE), jnp.max(depth[0]) - 1)]
        filler = jnp.zeros((128,), jnp.int32)
        rows = [filler] * 3 + [filler.at[:P_SIZE].set(own_row), filler, filler.at[:nodes].set(depth[0])]
        table = jnp.stack(rows + [filler] * 2)
        gathered = flood(cache, every, 1)
    blocks = gathered.reshape(branches * blk_dev, BT, width)
    return attend(queries, fresh, blocks, table, nodes, kv_dev, group_q)


def solution(mesh):
    placed = (
        P("branch", "tensor"),
        P("branch", None, None),
        P("branch", "tensor", None),
        P(),
        P("branch", None),
    )
    return jax.shard_map(
        body, mesh=mesh, in_specs=placed, out_specs=P("branch", "tensor"), check_vma=False
    )
```

```python
import functools
import math

import jax
import jax.numpy as jnp
from jax import lax
from jax.experimental import pallas as pl
from jax.experimental.pallas import tpu as pltpu
from jax.sharding import PartitionSpec as P

HQ = 64
KVH = 8
HD = 128
BT = 128
NODE_TOK = 128
P_SIZE = 48
STEP_BLOCKS = 4
K = 2
LAG = 3
RING = 4
LEAD = 4
LEVELS = (24, 26, 28, 30, 34, 42)
MESH = pl.DeviceIdType.MESH


def plan(zs, blk_dev, region, levels, parents, deep, me):
    n = 2 * zs
    nb = n * blk_dev
    big = 1 << 20
    i32 = jnp.int32
    listed = parents.shape[1]
    lane = lax.broadcasted_iota(i32, (n, listed), 1)
    act = jnp.where(lane < deep, parents, -1)
    blk = lax.broadcasted_iota(i32, (nb, listed), 0)
    need = []
    for z in range(zs):
        hit = (act[2 * z : 2 * z + 1, :] == blk) | (act[2 * z + 1 : 2 * z + 2, :] == blk)
        need.append(jnp.max(jnp.where(hit, 1, 0), axis=1, keepdims=True) > 0)
    bcol = lax.broadcasted_iota(i32, (nb, 1), 0)
    owner = jnp.zeros((nb, 1), i32)
    for o in range(1, n):
        owner = owner + jnp.where(bcol >= o * blk_dev, 1, 0)
    zb = owner >> 1
    cb = owner & 1
    eye = lax.broadcasted_iota(i32, (nb, nb), 0) == lax.broadcasted_iota(i32, (nb, nb), 1)

    def row(x):
        return jnp.sum(jnp.where(eye, x, 0), axis=0, keepdims=True)

    def rank(key):
        return jnp.sum(jnp.where(row(key) < key, 1, 0), axis=1, keepdims=True)

    def direction(fwd):
        zc = zb if fwd else zs - 1 - zb
        far = jnp.full((nb, 1), -1, i32)
        for z in range(zs):
            zz = z if fwd else zs - 1 - z
            far = jnp.where(need[z] & (zz > zc), jnp.maximum(far, zz), far)
        own_rank = jnp.full((nb, 1), big, i32)
        slots = []
        total = jnp.zeros((1, 1), i32)
        prev = jnp.zeros((nb, 1), i32)
        for k in range(zs - 1):
            own = (zc == k) & (far > k)
            rel = (zc < k) & (far > k)
            first = (cb * zs + (zs - far)) * nb + bcol
            key = jnp.where(own, first, jnp.where(rel, big + prev, 2 * big + bcol))
            key_row = row(key)
            r0 = jnp.sum(jnp.where(key_row < key, 1, 0), axis=1, keepdims=True)
            n0 = jnp.sum(jnp.where(own & (cb == 0), 1, 0), axis=0, keepdims=True)
            n1 = jnp.sum(jnp.where(own & (cb == 1), 1, 0), axis=0, keepdims=True)
            top = jnp.maximum(n0, n1)
            short = jnp.where(n0 <= n1, 0, 1)
            mine = r0 - cb * n0
            if k > 0:
                ready = (prev >> (K.bit_length())) + LAG
                at = jnp.where(ready * K <= top, top + ready * K, 2 * K * ready)
                gap_row = row(jnp.where(rel, at - r0, -big))
                gap = jnp.max(jnp.where(key_row <= key, gap_row, -big), axis=1, keepdims=True)
                r = r0 + jnp.maximum(gap, 0)
            else:
                r = r0
            far_slot = jnp.where(r < 2 * top, 2 * (r - top) + short, r)
            q = jnp.where(own, 2 * mine + cb, jnp.where(rel, far_slot, -1))
            own_rank = jnp.where(own, mine, own_rank)
            total = jnp.maximum(total, jnp.max(q, axis=0, keepdims=True) + 1)
            slots.append(q)
            prev = jnp.maximum(q, 0)
        return slots, own_rank, total

    right, rank_r, total_r = direction(True)
    left, rank_l, total_l = direction(False)
    local = jnp.zeros((nb, 1), jnp.bool_)
    for z in range(zs):
        local = local | (need[z] & (zb == z))
    key = jnp.minimum(2 * rank_r, 2 * rank_l + 1)
    key = jnp.where(key < big, key, jnp.where(local, big // 2 + bcol, big + bcol))
    order = rank(owner * (4 * big) + key) - owner * blk_dev

    me_z = me // 2
    me_c = me % 2
    lanes = lax.broadcasted_iota(i32, (1, 128), 1)

    def table(where_col, value_col):
        return jnp.sum(jnp.where(where_col == lanes, value_col, 0), axis=0, keepdims=True)

    def pick_link(slots, k):
        q = jnp.full((nb, 1), -1, i32)
        for j in range(zs - 1):
            q = jnp.where(k == j, slots[j], q)
        return q

    mine = owner == me
    picks = table(jnp.where(mine, order, -1), bcol - owner * blk_dev)

    def sources(slots, k):
        q = pick_link(slots, k)
        came = pick_link(slots, k - 1)
        source = jnp.where(zb == me_z, order, blk_dev + came)
        use = (q >= 0) & ((q & 1) == me_c)
        return table(jnp.where(use, q >> 1, -1), source)

    sel_r = sources(right, me_z)
    sel_l = sources(left, zs - 1 - me_z)
    from_r = pick_link(right, me_z - 1)
    from_l = pick_link(left, zs - 2 - me_z)
    place = jnp.where(
        zb == me_z,
        2 * order + cb,
        jnp.where(zb < me_z, 2 * blk_dev + from_r, 2 * (blk_dev + region) + from_l),
    )
    slot_count = (jnp.maximum(total_r, total_l) + 1) >> 1
    choice = jnp.zeros((1, 1), i32)
    for c in levels:
        choice = choice + jnp.where(slot_count > c, 1, 0)
    place = jnp.where(choice == len(levels), bcol, place)
    groups = lax.broadcasted_iota(i32, (n, listed), 0)
    my_row = jnp.sum(jnp.where(groups == me, act, 0), axis=0, keepdims=True)
    last = jnp.sum(jnp.where((groups == me) & (lane == deep - 1), act, 0), axis=(0, 1), keepdims=True)
    my_row = jnp.where(my_row < 0, last, my_row)
    pos = jnp.sum(jnp.where(bcol == my_row, place, 0), axis=0, keepdims=True)
    return picks, sel_r, sel_l, pos, choice, slot_count


def plan_kernel(zs, blk_dev, region, parents_ref, mine_ref, table_ref, all_ref, send_sem, recv_sem):
    n = 2 * zs
    me = lax.axis_index("branch")
    barrier = pltpu.get_barrier_semaphore()

    def greet(i, carry):
        peer = lax.rem(me + i, n)
        pl.semaphore_signal(barrier, inc=1, device_id={"branch": peer}, device_id_type=MESH)
        return carry

    lax.fori_loop(1, n, greet, 0)
    pl.semaphore_wait(barrier, n - 1)

    def copy(i):
        return pltpu.make_async_remote_copy(
            src_ref=mine_ref,
            dst_ref=all_ref.at[me],
            send_sem=send_sem.at[i],
            recv_sem=recv_sem.at[i],
            device_id={"branch": lax.rem(me + i, n)},
            device_id_type=MESH,
        )

    def start(i, carry):
        copy(i).start()
        return carry

    def finish(i, carry):
        copy(i).wait()
        return carry

    lax.fori_loop(1, n, start, 0)
    all_ref[pl.ds(me, 1)] = mine_ref[...][None]
    lax.fori_loop(1, n, finish, 0)
    deep = jnp.concatenate([jnp.max(all_ref[g, 0:1, :], axis=1, keepdims=True) for g in range(n)], axis=0)
    picks, sel_r, sel_l, pos, choice, _ = plan(
        zs, blk_dev, region, LEVELS, parents_ref[...], deep, me
    )
    table_ref[0:1, :] = picks
    table_ref[1:2, :] = sel_r
    table_ref[2:3, :] = sel_l
    table_ref[3:4, 0 : pos.shape[1]] = pos
    table_ref[4:5, :] = jnp.broadcast_to(choice, (1, 128))
    table_ref[5:6, :] = mine_ref[0:1, :]


def make_plan(parents, depth, n, blk_dev, region):
    nodes = depth.shape[1]
    mine = jnp.pad(depth, ((0, 7), (0, 128 - nodes)))
    return pl.pallas_call(
        functools.partial(plan_kernel, n // 2, blk_dev, region),
        out_shape=jax.ShapeDtypeStruct((8, 128), jnp.int32),
        in_specs=[pl.BlockSpec(memory_space=pltpu.VMEM)] * 2,
        out_specs=pl.BlockSpec(memory_space=pltpu.VMEM),
        scratch_shapes=[
            pltpu.VMEM((n, 8, 128), jnp.int32),
            pltpu.SemaphoreType.DMA((n,)),
            pltpu.SemaphoreType.DMA((n,)),
        ],
        compiler_params=pltpu.CompilerParams(collective_id=0, has_side_effects=True),
    )(parents, mine)


def pack_kernel(first_cols, width, pick_ref, block_ref, packed_ref):
    for t, first in enumerate(first_cols):
        packed_ref[t, 0] = block_ref[0, :, first : first + width]


def pack(cache, picks, count, first_cols, width):
    rows = cache.shape[1]
    tensors = len(first_cols)
    return pl.pallas_call(
        functools.partial(pack_kernel, first_cols, width),
        out_shape=jax.ShapeDtypeStruct((tensors, count, rows, width), cache.dtype),
        grid_spec=pltpu.PrefetchScalarGridSpec(
            num_scalar_prefetch=1,
            grid=(count,),
            in_specs=[pl.BlockSpec((1, rows, cache.shape[2]), lambda i, pick: (pick[i], 0, 0))],
            out_specs=pl.BlockSpec((tensors, 1, rows, width), lambda i, pick: (0, i, 0, 0)),
        ),
    )(picks, cache)


def spread_kernel(branches, tensors, count, chunk, packed_ref, out_ref, tp_send, tp_recv, own_sem,
                  right_send, right_recv, left_send, left_recv, pair_send, pair_recv):
    me_b = lax.axis_index("branch")
    me_t = lax.axis_index("tensor")
    z = me_b // 2
    depth_z = branches // 2
    partner = me_b + 1 - 2 * (me_b % 2)
    chunks = count // chunk
    has_left = z > 0
    has_right = z < depth_z - 1
    barrier = pltpu.get_barrier_semaphore()
    for step in range(1, tensors):
        pl.semaphore_signal(
            barrier, inc=1, device_id={"tensor": lax.rem(me_t + step, tensors)}, device_id_type=MESH
        )
    pl.semaphore_signal(barrier, inc=1, device_id={"branch": partner}, device_id_type=MESH)

    @pl.when(has_left)
    def _():
        pl.semaphore_signal(barrier, inc=1, device_id={"branch": me_b - 2}, device_id_type=MESH)

    @pl.when(has_right)
    def _():
        pl.semaphore_signal(barrier, inc=1, device_id={"branch": me_b + 2}, device_id_type=MESH)

    pl.semaphore_wait(barrier, tensors + jnp.minimum(z, 1) + jnp.minimum(depth_z - 1 - z, 1))

    def span(c):
        return pl.ds(c * chunk, chunk)

    def tensor_copy(step, c):
        to = lax.rem(me_t + step, tensors)
        return pltpu.make_async_remote_copy(
            src_ref=packed_ref.at[to, span(c)],
            dst_ref=out_ref.at[me_b, span(c), me_t],
            send_sem=tp_send.at[step - 1, c],
            recv_sem=tp_recv.at[step - 1, c],
            device_id={"tensor": to},
            device_id_type=MESH,
        )

    def own_copy(c):
        return pltpu.make_async_copy(
            packed_ref.at[me_t, span(c)], out_ref.at[me_b, span(c), me_t], own_sem.at[c]
        )

    def lane_copy(origin, c, target, send_sem, recv_sem):
        return pltpu.make_async_remote_copy(
            src_ref=out_ref.at[origin, span(c)],
            dst_ref=out_ref.at[origin, span(c)],
            send_sem=send_sem,
            recv_sem=recv_sem,
            device_id={"branch": target},
            device_id_type=MESH,
        )

    def to_right(h, c):
        return lane_copy(me_b - 2 * h, c, me_b + 2, right_send.at[h, c], right_recv.at[h + 1, c])

    def from_left(h, c):
        return lane_copy(me_b - 2 * h, c, me_b, right_send.at[h, c], right_recv.at[h, c])

    def to_left(h, c):
        return lane_copy(me_b + 2 * h, c, me_b - 2, left_send.at[h, c], left_recv.at[h + 1, c])

    def from_right(h, c):
        return lane_copy(me_b + 2 * h, c, me_b, left_send.at[h, c], left_recv.at[h, c])

    def to_pair(origin, c):
        return lane_copy(origin, c, partner, pair_send.at[origin // 2, c], pair_recv.at[origin // 2, c])

    def from_pair(origin_z, c):
        origin = origin_z * 2 + 1 - (me_b % 2)
        return lane_copy(origin, c, partner, pair_send.at[origin_z, c], pair_recv.at[origin_z, c])

    def start_tensor(c, carry):
        own_copy(c).start()
        for step in range(1, tensors):
            tensor_copy(step, c).start()
        return carry

    lax.fori_loop(0, chunks, start_tensor, 0)

    def advance(s, carry):
        @pl.when(s < chunks)
        def _():
            for step in range(1, tensors):
                tensor_copy(step, s).wait_recv()
            own_copy(s).wait()

            @pl.when(has_right)
            def _():
                to_right(0, s).start()

            @pl.when(has_left)
            def _():
                to_left(0, s).start()

            to_pair(me_b, s).start()

        for h in range(1, depth_z):
            c = s - h
            in_range = jnp.logical_and(c >= 0, c < chunks)

            @pl.when(jnp.logical_and(in_range, z - h >= 0))
            def _():
                from_left(h, c).wait_recv()

                @pl.when(has_right)
                def _():
                    to_right(h, c).start()

                to_pair(me_b - 2 * h, c).start()

            @pl.when(jnp.logical_and(in_range, z + h < depth_z))
            def _():
                from_right(h, c).wait_recv()

                @pl.when(has_left)
                def _():
                    to_left(h, c).start()

                to_pair(me_b + 2 * h, c).start()

        return carry

    lax.fori_loop(0, chunks + depth_z - 1, advance, 0)

    def finish(c, carry):
        for step in range(1, tensors):
            tensor_copy(step, c).wait_send()
        for h in range(depth_z):
            from_pair(h, c).wait_recv()
            to_pair(h * 2 + (me_b % 2), c).wait_send()

            @pl.when(jnp.logical_and(has_right, z - h >= 0))
            def _():
                to_right(h, c).wait_send()

            @pl.when(jnp.logical_and(has_left, z + h < depth_z))
            def _():
                to_left(h, c).wait_send()

        return carry

    lax.fori_loop(0, chunks, finish, 0)


def spread(packed, branches, blk_dev, collective):
    tensors, count, rows, width = packed.shape
    depth_z = branches // 2
    chunk = max(1, count // (8 if depth_z <= 4 else 2))
    while count % chunk:
        chunk -= 1
    chunks = count // chunk
    dma = pltpu.SemaphoreType.DMA
    return pl.pallas_call(
        functools.partial(spread_kernel, branches, tensors, count, chunk),
        out_shape=jax.ShapeDtypeStruct((branches, blk_dev, tensors, rows, width), packed.dtype),
        in_specs=[pl.BlockSpec(memory_space=pltpu.VMEM)],
        out_specs=pl.BlockSpec(memory_space=pl.ANY),
        scratch_shapes=[
            dma((tensors - 1, chunks)),
            dma((tensors - 1, chunks)),
            dma((chunks,)),
        ]
        + [dma((depth_z, chunks))] * 6,
        compiler_params=pltpu.CompilerParams(collective_id=collective, has_side_effects=True),
    )(packed)


def relay_kernel(zs, tensors, blk_dev, region, count, first_cols, width, tab_ref, stored_ref, out_ref,
                 cache_ref, cache_sem, stage, landed, pool_x, in_r, in_l, pool_r, pool_l, ring_r, ring_l,
                 x_send, x_recv, x_own, x_psend, x_precv, x_keep,
                 r_send, r_recv, rp_send, rp_recv, r_keep,
                 l_send, l_recv, lp_send, lp_recv, l_keep):
    me_b = lax.axis_index("branch")
    me_t = lax.axis_index("tensor")
    z = me_b // 2
    core = lax.rem(me_b, 2)
    other = 1 - core
    partner = me_b + 1 - 2 * core
    has_left = z > 0
    has_right = z < zs - 1
    group = 2 * K
    pieces = blk_dev // group
    chunks = count // K
    load = pltpu.make_async_copy(stored_ref, cache_ref, cache_sem)
    load.start()
    barrier = pltpu.get_barrier_semaphore()
    for step in range(1, tensors):
        pl.semaphore_signal(
            barrier, inc=1, device_id={"tensor": lax.rem(me_t + step, tensors)}, device_id_type=MESH
        )
    pl.semaphore_signal(barrier, inc=1, device_id={"branch": partner}, device_id_type=MESH)

    @pl.when(has_left)
    def _():
        pl.semaphore_signal(barrier, inc=1, device_id={"branch": me_b - 2}, device_id_type=MESH)

    @pl.when(has_right)
    def _():
        pl.semaphore_signal(barrier, inc=1, device_id={"branch": me_b + 2}, device_id_type=MESH)

    pl.semaphore_wait(barrier, tensors + jnp.minimum(z, 1) + jnp.minimum(zs - 1 - z, 1))

    def x_span(x):
        return pl.ds(x * group, group)

    def span(c):
        return pl.ds(c * K, K)

    def share(step, x):
        to = lax.rem(me_t + step, tensors)
        return pltpu.make_async_remote_copy(
            src_ref=stage.at[to, x_span(x)],
            dst_ref=landed.at[x_span(x), me_t],
            send_sem=x_send.at[step - 1, x],
            recv_sem=x_recv.at[step - 1, x],
            device_id={"tensor": to},
            device_id_type=MESH,
        )

    def own_part(x):
        return pltpu.make_async_copy(
            stage.at[me_t, x_span(x)], landed.at[x_span(x), me_t], x_own.at[x]
        )

    def x_pair(x):
        return pltpu.make_async_remote_copy(
            src_ref=landed.at[x_span(x)],
            dst_ref=out_ref.at[x_span(x), core],
            send_sem=x_psend.at[x],
            recv_sem=x_precv.at[x],
            device_id={"branch": partner},
            device_id_type=MESH,
        )

    def x_local(x):
        return pltpu.make_async_copy(landed.at[x_span(x)], out_ref.at[x_span(x), core], x_keep.at[x])

    def send(ring, into, target, send_sem, recv_sem, c):
        return pltpu.make_async_remote_copy(
            src_ref=ring.at[span(lax.rem(c, RING))],
            dst_ref=into.at[span(c), core],
            send_sem=send_sem.at[c],
            recv_sem=recv_sem.at[c],
            device_id={"branch": target},
            device_id_type=MESH,
        )

    def pair(into, send_sem, recv_sem, c):
        return pltpu.make_async_remote_copy(
            src_ref=into.at[span(c), core],
            dst_ref=into.at[span(c), core],
            send_sem=send_sem.at[c],
            recv_sem=recv_sem.at[c],
            device_id={"branch": partner},
            device_id_type=MESH,
        )

    def keep(into, base, lane, keep_sem, c):
        return pltpu.make_async_copy(
            into.at[span(c), lane], out_ref.at[pl.ds(base + c * K, K), lane], keep_sem.at[lane, c]
        )

    flows = (
        (1, ring_r, in_r, pool_r, me_b + 2, has_right, has_left, r_send, r_recv, rp_send, rp_recv,
         r_keep, blk_dev),
        (2, ring_l, in_l, pool_l, me_b - 2, has_left, has_right, l_send, l_recv, lp_send, lp_recv,
         l_keep, blk_dev + region),
    )

    def prepare(x):
        def one(j, carry):
            block = tab_ref[0, x * group + j]
            for t, first in enumerate(first_cols):
                stage[t, x * group + j] = cache_ref[block, :, first : first + width]
            return carry

        lax.fori_loop(0, group, one, 0)
        for step in range(1, tensors):
            share(step, x).start()
        own_part(x).start()

    load.wait()
    for x in range(min(LEAD, pieces)):
        prepare(x)

    def advance(s, carry):
        @pl.when(s + LEAD < pieces)
        def _():
            prepare(s + LEAD)

        @pl.when(s < pieces)
        def _():
            for step in range(1, tensors):
                share(step, s).wait_recv()
            own_part(s).wait()
            x_pair(s).start()
            x_local(s).start()

            def one(j, carry):
                pool_x[s * group + j] = landed[s * group + j]
                return carry

            lax.fori_loop(0, group, one, 0)

        for row, ring, into, pool, target, sends, takes, ssem, rsem, pssem, prsem, ksem, base in flows:
            c = s - LAG

            @pl.when(jnp.logical_and(takes, jnp.logical_and(c >= 0, c < chunks)))
            def _():
                pair(into, pssem, prsem, c).wait_recv()
                keep(into, base, other, ksem, c).start()

                def one(j, carry):
                    pool[2 * (c * K + j)] = into[c * K + j, 0]
                    pool[2 * (c * K + j) + 1] = into[c * K + j, 1]
                    return carry

                lax.fori_loop(0, K, one, 0)

        for row, ring, into, pool, target, sends, takes, ssem, rsem, pssem, prsem, ksem, base in flows:

            @pl.when(jnp.logical_and(sends, s < chunks))
            def _():
                @pl.when(s >= RING)
                def _():
                    send(ring, into, target, ssem, rsem, s - RING).wait_send()

                def one(j, carry):
                    source = tab_ref[row, s * K + j]
                    near = pool_x[jnp.minimum(source, blk_dev - 1)]
                    far = pool[jnp.clip(source - blk_dev, 0, 2 * count - 1)]
                    ring[lax.rem(s, RING) * K + j] = jnp.where(source < blk_dev, near, far)
                    return carry

                lax.fori_loop(0, K, one, 0)
                send(ring, into, target, ssem, rsem, s).start()

        for row, ring, into, pool, target, sends, takes, ssem, rsem, pssem, prsem, ksem, base in flows:
            c = s - LAG + 1

            @pl.when(jnp.logical_and(takes, jnp.logical_and(c >= 0, c < chunks)))
            def _():
                send(ring, into, me_b, ssem, rsem, c).wait_recv()
                pair(into, pssem, prsem, c).start()
                keep(into, base, core, ksem, c).start()

        return carry

    lax.fori_loop(0, max(chunks + LAG, pieces), advance, 0)

    def finish_x(x, carry):
        for step in range(1, tensors):
            share(step, x).wait_send()
        x_pair(x).wait()
        x_local(x).wait()
        return carry

    lax.fori_loop(0, pieces, finish_x, 0)

    def finish(c, carry):
        for row, ring, into, pool, target, sends, takes, ssem, rsem, pssem, prsem, ksem, base in flows:

            @pl.when(takes)
            def _():
                pair(into, pssem, prsem, c).wait_send()
                keep(into, base, 0, ksem, c).wait()
                keep(into, base, 1, ksem, c).wait()

            @pl.when(jnp.logical_and(sends, c >= chunks - RING))
            def _():
                send(ring, into, target, ssem, rsem, c).wait_send()

        return carry

    lax.fori_loop(0, chunks, finish, 0)


def relay(table, cache, zs, tensors, count, region, first_cols, width, collective):
    blk_dev, rows, _ = cache.shape
    total = 2 * zs * blk_dev
    dma = pltpu.SemaphoreType.DMA
    pieces = blk_dev // (2 * K)
    chunks = count // K
    block = (tensors, rows, width)
    flow = [dma((chunks,))] * 4 + [dma((2, chunks))]
    return pl.pallas_call(
        functools.partial(
            relay_kernel, zs, tensors, blk_dev, region, count, first_cols, width
        ),
        out_shape=jax.ShapeDtypeStruct((total // 2, 2) + block, cache.dtype),
        in_specs=[pl.BlockSpec(memory_space=pltpu.SMEM), pl.BlockSpec(memory_space=pl.ANY)],
        out_specs=pl.BlockSpec(memory_space=pl.ANY),
        scratch_shapes=[
            pltpu.VMEM(cache.shape, cache.dtype),
            dma,
            pltpu.VMEM((tensors, blk_dev, rows, width), cache.dtype),
            pltpu.VMEM((blk_dev,) + block, cache.dtype),
            pltpu.VMEM((blk_dev,) + block, cache.dtype),
            pltpu.VMEM((count, 2) + block, cache.dtype),
            pltpu.VMEM((count, 2) + block, cache.dtype),
            pltpu.VMEM((2 * count,) + block, cache.dtype),
            pltpu.VMEM((2 * count,) + block, cache.dtype),
            pltpu.VMEM((RING * K,) + block, cache.dtype),
            pltpu.VMEM((RING * K,) + block, cache.dtype),
            dma((tensors - 1, pieces)),
            dma((tensors - 1, pieces)),
        ]
        + [dma((pieces,))] * 4
        + flow
        + flow,
        compiler_params=pltpu.CompilerParams(
            collective_id=collective, has_side_effects=True, vmem_limit_bytes=62 * 2**20
        ),
    )(table, cache)


def attend_kernel(nodes, kv_dev, group_q, tab_ref, q_ref, fresh_ref, *refs):
    kv_refs = refs[:STEP_BLOCKS]
    out_ref, q_s, m_s, l_s, acc_s = refs[STEP_BLOCKS:]
    i = pl.program_id(0)
    factor = math.log2(math.e) / math.sqrt(HD)
    rows = group_q * NODE_TOK
    tile = min(rows, 256)
    contract = (((1,), (1,)), ((), ()))

    @pl.when(i == 0)
    def _():
        row = lax.broadcasted_iota(jnp.int32, (NODE_TOK, NODE_TOK), 0)
        col = lax.broadcasted_iota(jnp.int32, (NODE_TOK, NODE_TOK), 1)
        for n in range(nodes):
            tok = slice(n * NODE_TOK, (n + 1) * NODE_TOK)
            for h in range(kv_dev):
                k = fresh_ref[tok, h * 2 * HD : h * 2 * HD + HD]
                v = fresh_ref[tok, h * 2 * HD + HD : (h + 1) * 2 * HD]
                for a in range(group_q):
                    head = h * group_q + a
                    here = slice(a * NODE_TOK, (a + 1) * NODE_TOK)
                    q = q_ref[tok, head * HD : (head + 1) * HD]
                    wide_q = q.astype(jnp.float32) * factor
                    upper = wide_q.astype(jnp.bfloat16)
                    q_s[n * kv_dev + h, here, :HD] = upper
                    q_s[n * kv_dev + h, here, HD:] = (wide_q - upper.astype(jnp.float32)).astype(jnp.bfloat16)
                    s = lax.dot_general(q, k, contract, preferred_element_type=jnp.float32)
                    s = jnp.where(col <= row, s * factor, -jnp.inf)
                    m = jnp.max(s, axis=1, keepdims=True)
                    w = jnp.exp2(s - m)
                    m_s[n * kv_dev + h, here, :] = jnp.broadcast_to(m, (NODE_TOK, 128))
                    l_s[n * kv_dev + h, here, :] = jnp.broadcast_to(jnp.sum(w, axis=1, keepdims=True), (NODE_TOK, 128))
                    acc_s[n * kv_dev + h, here, :] = jnp.dot(
                        w.astype(jnp.bfloat16), v, preferred_element_type=jnp.float32
                    )

    def visit(n, masked):
        keys = STEP_BLOCKS * BT
        if masked:
            slot = lax.broadcasted_iota(jnp.int32, (1, keys), 1) // BT + i * STEP_BLOCKS
            seen = slot < tab_ref[5, n]
        for h in range(kv_dev):
            k = jnp.concatenate([r[0, :, h * 2 * HD : h * 2 * HD + HD] for r in kv_refs], axis=0)
            v = jnp.concatenate([r[0, :, h * 2 * HD + HD : (h + 1) * 2 * HD] for r in kv_refs], axis=0)
            vv = jnp.concatenate([v, jnp.ones_like(v)], axis=1)
            kk = jnp.concatenate([k, k], axis=1)
            p = n * kv_dev + h
            for start in range(0, rows, tile):
                here = slice(start, start + tile)
                s = lax.dot_general(
                    q_s[p, here, :], kk, contract, preferred_element_type=jnp.float32
                )
                if masked:
                    s = jnp.where(seen, s, -jnp.inf)
                m_old = m_s[p, here, :]
                m_new = jnp.maximum(m_old, jnp.max(s, axis=1, keepdims=True))
                alpha = jnp.exp2(m_old - m_new)
                w = [jnp.exp2(s[:, u * 128 : (u + 1) * 128] - m_new) for u in range(keys // 128)]
                wide = jnp.concatenate([x.astype(jnp.bfloat16) for x in w], axis=1)
                both = jnp.dot(wide, vv, preferred_element_type=jnp.float32)
                acc_s[p, here, :] = acc_s[p, here, :] * alpha + both[:, :HD]
                l_s[p, here, :] = l_s[p, here, :] * alpha + both[:, HD:]
                m_s[p, here, :] = m_new

    for n in range(nodes):
        first = i * STEP_BLOCKS
        whole = first + STEP_BLOCKS <= tab_ref[5, n]

        @pl.when(whole)
        def _():
            visit(n, False)

        @pl.when(jnp.logical_and(first < tab_ref[5, n], jnp.logical_not(whole)))
        def _():
            visit(n, True)

    @pl.when(i == pl.num_programs(0) - 1)
    def _():
        for n in range(nodes):
            for h in range(kv_dev):
                p = n * kv_dev + h
                for a in range(group_q):
                    head = h * group_q + a
                    here = slice(a * NODE_TOK, (a + 1) * NODE_TOK)
                    total = l_s[p, here, :]
                    out_ref[n * NODE_TOK : (n + 1) * NODE_TOK, head * HD : (head + 1) * HD] = (
                        acc_s[p, here, :] / total
                    ).astype(out_ref.dtype)


def attend(queries, fresh, blocks, table, nodes, kv_dev, group_q):
    new_rows, q_cols = queries.shape
    width = blocks.shape[2]
    rows = group_q * NODE_TOK
    pairs = nodes * kv_dev

    def kv_spec(u):
        return pl.BlockSpec((1, BT, width), lambda i, tab: (tab[3, i * STEP_BLOCKS + u], 0, 0))

    return pl.pallas_call(
        functools.partial(attend_kernel, nodes, kv_dev, group_q),
        out_shape=jax.ShapeDtypeStruct((new_rows, q_cols), queries.dtype),
        grid_spec=pltpu.PrefetchScalarGridSpec(
            num_scalar_prefetch=1,
            grid=(P_SIZE // STEP_BLOCKS,),
            in_specs=[
                pl.BlockSpec((new_rows, q_cols), lambda i, tab: (0, 0)),
                pl.BlockSpec((new_rows, width), lambda i, tab: (0, 0)),
            ]
            + [kv_spec(u) for u in range(STEP_BLOCKS)],
            out_specs=pl.BlockSpec((new_rows, q_cols), lambda i, tab: (0, 0)),
            scratch_shapes=[
                pltpu.VMEM((pairs, rows, 2 * HD), jnp.bfloat16),
                pltpu.VMEM((pairs, rows, 128), jnp.float32),
                pltpu.VMEM((pairs, rows, 128), jnp.float32),
                pltpu.VMEM((pairs, rows, HD), jnp.float32),
            ],
        ),
        compiler_params=pltpu.CompilerParams(vmem_limit_bytes=48 * 2**20),
    )(table, queries, fresh, *([blocks] * STEP_BLOCKS))


def body(queries, new_kv, cache, parents, depth):
    tensor_size = lax.axis_size("tensor")
    branches = lax.axis_size("branch")
    tensor_pos = lax.axis_index("tensor")
    branch_pos = lax.axis_index("branch")
    sharing = HQ // KVH
    heads_dev = queries.shape[1] // HD
    kv_dev = max(1, heads_dev // sharing)
    group_q = heads_dev // kv_dev
    first_kv = tensor_pos * heads_dev // sharing
    blk_dev = cache.shape[0]
    new_rows = queries.shape[0]
    width = kv_dev * 2 * HD
    nodes = depth.shape[1]
    zs = branches // 2
    first_cols = [(t * heads_dev // sharing) * 2 * HD for t in range(tensor_size)]
    fresh = lax.dynamic_slice_in_dim(new_kv, first_kv, kv_dev, 1).reshape(new_rows, width)
    out_blocks = (branches * blk_dev // 2, 2, tensor_size, cache.shape[1], width)

    def flood(cache, picks, collective):
        packed = pack(cache, picks, blk_dev, first_cols, width)
        return spread(packed, branches, blk_dev, collective).reshape(out_blocks)

    region = (branches * blk_dev - 2 * blk_dev) // 4
    every = jnp.arange(blk_dev, dtype=jnp.int32)
    if zs <= 4 and blk_dev % (2 * K) == 0 and region >= LEVELS[-1] and branches * blk_dev <= 256:
        table = make_plan(parents, depth, branches, blk_dev, region)

        def with_count(count, collective):
            def run(table, cache):
                return relay(
                    table, cache, zs, tensor_size, count, region, first_cols, width, collective
                )

            return run

        runs = [with_count(count, 1 + i) for i, count in enumerate(LEVELS)]
        runs.append(lambda table, cache: flood(cache, every, 1 + len(LEVELS)))
        gathered = lax.switch(table[4, 0], runs, table, cache)
    else:
        own_row = lax.dynamic_index_in_dim(parents, branch_pos, 0, keepdims=False)
        own_row = own_row[jnp.minimum(jnp.arange(P_SIZE), jnp.max(depth[0]) - 1)]
        filler = jnp.zeros((128,), jnp.int32)
        rows = [filler] * 3 + [filler.at[:P_SIZE].set(own_row), filler, filler.at[:nodes].set(depth[0])]
        table = jnp.stack(rows + [filler] * 2)
        gathered = flood(cache, every, 1)
    blocks = gathered.reshape(branches * blk_dev, BT, width)
    return attend(queries, fresh, blocks, table, nodes, kv_dev, group_q)


def solution(mesh):
    placed = (
        P("branch", "tensor"),
        P("branch", None, None),
        P("branch", "tensor", None),
        P(),
        P("branch", None),
    )
    return jax.shard_map(
        body, mesh=mesh, in_specs=placed, out_specs=P("branch", "tensor"), check_vma=False
    )
```

```python
import functools
import math

import jax
import jax.numpy as jnp
from jax import lax
from jax.experimental import pallas as pl
from jax.experimental.pallas import tpu as pltpu
from jax.sharding import PartitionSpec as P

HQ = 64
KVH = 8
HD = 128
BT = 128
NODE_TOK = 128
P_SIZE = 48
STEP_BLOCKS = 4
K = 1
LAG = 4
ARRIVE = 2
RING = 6
LEAD = 6
LEVELS = (22, 24, 26, 28, 30, 32, 35, 42)
MESH = pl.DeviceIdType.MESH


def plan(zs, blk_dev, region, levels, parents, deep, me):
    n = 2 * zs
    nb = n * blk_dev
    big = 1 << 20
    i32 = jnp.int32
    listed = parents.shape[1]
    lane = lax.broadcasted_iota(i32, (n, listed), 1)
    act = jnp.where(lane < deep, parents, -1)
    blk = lax.broadcasted_iota(i32, (nb, listed), 0)
    need = []
    for z in range(zs):
        hit = (act[2 * z : 2 * z + 1, :] == blk) | (act[2 * z + 1 : 2 * z + 2, :] == blk)
        need.append(jnp.max(jnp.where(hit, 1, 0), axis=1, keepdims=True) > 0)
    bcol = lax.broadcasted_iota(i32, (nb, 1), 0)
    owner = jnp.zeros((nb, 1), i32)
    for o in range(1, n):
        owner = owner + jnp.where(bcol >= o * blk_dev, 1, 0)
    zb = owner >> 1
    cb = owner & 1
    eye = lax.broadcasted_iota(i32, (nb, nb), 0) == lax.broadcasted_iota(i32, (nb, nb), 1)

    def row(x):
        return jnp.sum(jnp.where(eye, x, 0), axis=0, keepdims=True)

    def rank(key):
        return jnp.sum(jnp.where(row(key) < key, 1, 0), axis=1, keepdims=True)

    def direction(fwd):
        zc = zb if fwd else zs - 1 - zb
        far = jnp.full((nb, 1), -1, i32)
        for z in range(zs):
            zz = z if fwd else zs - 1 - z
            far = jnp.where(need[z] & (zz > zc), jnp.maximum(far, zz), far)
        own_rank = jnp.full((nb, 1), big, i32)
        slots = []
        total = jnp.zeros((1, 1), i32)
        prev = jnp.zeros((nb, 1), i32)
        for k in range(zs - 1):
            own = (zc == k) & (far > k)
            rel = (zc < k) & (far > k)
            first = (cb * zs + (zs - far)) * nb + bcol
            key = jnp.where(own, first, jnp.where(rel, big + prev, 2 * big + bcol))
            key_row = row(key)
            r0 = jnp.sum(jnp.where(key_row < key, 1, 0), axis=1, keepdims=True)
            n0 = jnp.sum(jnp.where(own & (cb == 0), 1, 0), axis=0, keepdims=True)
            n1 = jnp.sum(jnp.where(own & (cb == 1), 1, 0), axis=0, keepdims=True)
            top = jnp.maximum(n0, n1)
            short = jnp.where(n0 <= n1, 0, 1)
            mine = r0 - cb * n0
            if k > 0:
                ready = (prev >> (K.bit_length())) + LAG
                at = jnp.where(ready * K <= top, top + ready * K, 2 * K * ready)
                gap_row = row(jnp.where(rel, at - r0, -big))
                gap = jnp.max(jnp.where(key_row <= key, gap_row, -big), axis=1, keepdims=True)
                r = r0 + jnp.maximum(gap, 0)
            else:
                r = r0
            far_slot = jnp.where(r < 2 * top, 2 * (r - top) + short, r)
            q = jnp.where(own, 2 * mine + cb, jnp.where(rel, far_slot, -1))
            own_rank = jnp.where(own, mine, own_rank)
            total = jnp.maximum(total, jnp.max(q, axis=0, keepdims=True) + 1)
            slots.append(q)
            prev = jnp.maximum(q, 0)
        return slots, own_rank, total

    right, rank_r, total_r = direction(True)
    left, rank_l, total_l = direction(False)
    local = jnp.zeros((nb, 1), jnp.bool_)
    for z in range(zs):
        local = local | (need[z] & (zb == z))
    key = jnp.minimum(2 * rank_r, 2 * rank_l + 1)
    key = jnp.where(key < big, key, jnp.where(local, big // 2 + bcol, big + bcol))
    order = rank(owner * (4 * big) + key) - owner * blk_dev

    me_z = me // 2
    me_c = me % 2
    lanes = lax.broadcasted_iota(i32, (1, 128), 1)

    def table(where_col, value_col):
        return jnp.sum(jnp.where(where_col == lanes, value_col, 0), axis=0, keepdims=True)

    def pick_link(slots, k):
        q = jnp.full((nb, 1), -1, i32)
        for j in range(zs - 1):
            q = jnp.where(k == j, slots[j], q)
        return q

    mine = owner == me
    picks = table(jnp.where(mine, order, -1), bcol - owner * blk_dev)

    def sources(slots, k):
        q = pick_link(slots, k)
        came = pick_link(slots, k - 1)
        source = jnp.where(zb == me_z, order, blk_dev + came)
        use = (q >= 0) & ((q & 1) == me_c)
        return table(jnp.where(use, q >> 1, -1), source)

    sel_r = sources(right, me_z)
    sel_l = sources(left, zs - 1 - me_z)
    from_r = pick_link(right, me_z - 1)
    from_l = pick_link(left, zs - 2 - me_z)
    place = jnp.where(
        zb == me_z,
        2 * order + cb,
        jnp.where(zb < me_z, 2 * blk_dev + from_r, 2 * (blk_dev + region) + from_l),
    )
    slot_count = (jnp.maximum(total_r, total_l) + 1) >> 1
    choice = jnp.zeros((1, 1), i32)
    for c in levels:
        choice = choice + jnp.where(slot_count > c, 1, 0)
    place = jnp.where(choice == len(levels), bcol, place)
    groups = lax.broadcasted_iota(i32, (n, listed), 0)
    my_row = jnp.sum(jnp.where(groups == me, act, 0), axis=0, keepdims=True)
    last = jnp.sum(jnp.where((groups == me) & (lane == deep - 1), act, 0), axis=(0, 1), keepdims=True)
    my_row = jnp.where(my_row < 0, last, my_row)
    pos = jnp.sum(jnp.where(bcol == my_row, place, 0), axis=0, keepdims=True)
    return picks, sel_r, sel_l, pos, choice, slot_count


def plan_kernel(zs, blk_dev, region, parents_ref, mine_ref, table_ref, all_ref, send_sem, recv_sem):
    n = 2 * zs
    me = lax.axis_index("branch")
    barrier = pltpu.get_barrier_semaphore()

    def greet(i, carry):
        peer = lax.rem(me + i, n)
        pl.semaphore_signal(barrier, inc=1, device_id={"branch": peer}, device_id_type=MESH)
        return carry

    lax.fori_loop(1, n, greet, 0)
    pl.semaphore_wait(barrier, n - 1)

    def copy(i):
        return pltpu.make_async_remote_copy(
            src_ref=mine_ref,
            dst_ref=all_ref.at[me],
            send_sem=send_sem.at[i],
            recv_sem=recv_sem.at[i],
            device_id={"branch": lax.rem(me + i, n)},
            device_id_type=MESH,
        )

    def start(i, carry):
        copy(i).start()
        return carry

    def finish(i, carry):
        copy(i).wait()
        return carry

    lax.fori_loop(1, n, start, 0)
    all_ref[pl.ds(me, 1)] = mine_ref[...][None]
    lax.fori_loop(1, n, finish, 0)
    deep = jnp.concatenate([jnp.max(all_ref[g, 0:1, :], axis=1, keepdims=True) for g in range(n)], axis=0)
    picks, sel_r, sel_l, pos, choice, _ = plan(
        zs, blk_dev, region, LEVELS, parents_ref[...], deep, me
    )
    table_ref[0:1, :] = picks
    table_ref[1:2, :] = sel_r
    table_ref[2:3, :] = sel_l
    table_ref[3:4, 0 : pos.shape[1]] = pos
    table_ref[4:5, :] = jnp.broadcast_to(choice, (1, 128))
    table_ref[5:6, :] = mine_ref[0:1, :]


def make_plan(parents, depth, n, blk_dev, region):
    nodes = depth.shape[1]
    mine = jnp.pad(depth, ((0, 7), (0, 128 - nodes)))
    return pl.pallas_call(
        functools.partial(plan_kernel, n // 2, blk_dev, region),
        out_shape=jax.ShapeDtypeStruct((8, 128), jnp.int32),
        in_specs=[pl.BlockSpec(memory_space=pltpu.VMEM)] * 2,
        out_specs=pl.BlockSpec(memory_space=pltpu.VMEM),
        scratch_shapes=[
            pltpu.VMEM((n, 8, 128), jnp.int32),
            pltpu.SemaphoreType.DMA((n,)),
            pltpu.SemaphoreType.DMA((n,)),
        ],
        compiler_params=pltpu.CompilerParams(collective_id=0, has_side_effects=True),
    )(parents, mine)


def pack_kernel(first_cols, width, pick_ref, block_ref, packed_ref):
    for t, first in enumerate(first_cols):
        packed_ref[t, 0] = block_ref[0, :, first : first + width]


def pack(cache, picks, count, first_cols, width):
    rows = cache.shape[1]
    tensors = len(first_cols)
    return pl.pallas_call(
        functools.partial(pack_kernel, first_cols, width),
        out_shape=jax.ShapeDtypeStruct((tensors, count, rows, width), cache.dtype),
        grid_spec=pltpu.PrefetchScalarGridSpec(
            num_scalar_prefetch=1,
            grid=(count,),
            in_specs=[pl.BlockSpec((1, rows, cache.shape[2]), lambda i, pick: (pick[i], 0, 0))],
            out_specs=pl.BlockSpec((tensors, 1, rows, width), lambda i, pick: (0, i, 0, 0)),
        ),
    )(picks, cache)


def spread_kernel(branches, tensors, count, chunk, packed_ref, out_ref, tp_send, tp_recv, own_sem,
                  right_send, right_recv, left_send, left_recv, pair_send, pair_recv):
    me_b = lax.axis_index("branch")
    me_t = lax.axis_index("tensor")
    z = me_b // 2
    depth_z = branches // 2
    partner = me_b + 1 - 2 * (me_b % 2)
    chunks = count // chunk
    has_left = z > 0
    has_right = z < depth_z - 1
    barrier = pltpu.get_barrier_semaphore()
    for step in range(1, tensors):
        pl.semaphore_signal(
            barrier, inc=1, device_id={"tensor": lax.rem(me_t + step, tensors)}, device_id_type=MESH
        )
    pl.semaphore_signal(barrier, inc=1, device_id={"branch": partner}, device_id_type=MESH)

    @pl.when(has_left)
    def _():
        pl.semaphore_signal(barrier, inc=1, device_id={"branch": me_b - 2}, device_id_type=MESH)

    @pl.when(has_right)
    def _():
        pl.semaphore_signal(barrier, inc=1, device_id={"branch": me_b + 2}, device_id_type=MESH)

    pl.semaphore_wait(barrier, tensors + jnp.minimum(z, 1) + jnp.minimum(depth_z - 1 - z, 1))

    def span(c):
        return pl.ds(c * chunk, chunk)

    def tensor_copy(step, c):
        to = lax.rem(me_t + step, tensors)
        return pltpu.make_async_remote_copy(
            src_ref=packed_ref.at[to, span(c)],
            dst_ref=out_ref.at[me_b, span(c), me_t],
            send_sem=tp_send.at[step - 1, c],
            recv_sem=tp_recv.at[step - 1, c],
            device_id={"tensor": to},
            device_id_type=MESH,
        )

    def own_copy(c):
        return pltpu.make_async_copy(
            packed_ref.at[me_t, span(c)], out_ref.at[me_b, span(c), me_t], own_sem.at[c]
        )

    def lane_copy(origin, c, target, send_sem, recv_sem):
        return pltpu.make_async_remote_copy(
            src_ref=out_ref.at[origin, span(c)],
            dst_ref=out_ref.at[origin, span(c)],
            send_sem=send_sem,
            recv_sem=recv_sem,
            device_id={"branch": target},
            device_id_type=MESH,
        )

    def to_right(h, c):
        return lane_copy(me_b - 2 * h, c, me_b + 2, right_send.at[h, c], right_recv.at[h + 1, c])

    def from_left(h, c):
        return lane_copy(me_b - 2 * h, c, me_b, right_send.at[h, c], right_recv.at[h, c])

    def to_left(h, c):
        return lane_copy(me_b + 2 * h, c, me_b - 2, left_send.at[h, c], left_recv.at[h + 1, c])

    def from_right(h, c):
        return lane_copy(me_b + 2 * h, c, me_b, left_send.at[h, c], left_recv.at[h, c])

    def to_pair(origin, c):
        return lane_copy(origin, c, partner, pair_send.at[origin // 2, c], pair_recv.at[origin // 2, c])

    def from_pair(origin_z, c):
        origin = origin_z * 2 + 1 - (me_b % 2)
        return lane_copy(origin, c, partner, pair_send.at[origin_z, c], pair_recv.at[origin_z, c])

    def start_tensor(c, carry):
        own_copy(c).start()
        for step in range(1, tensors):
            tensor_copy(step, c).start()
        return carry

    lax.fori_loop(0, chunks, start_tensor, 0)

    def advance(s, carry):
        @pl.when(s < chunks)
        def _():
            for step in range(1, tensors):
                tensor_copy(step, s).wait_recv()
            own_copy(s).wait()

            @pl.when(has_right)
            def _():
                to_right(0, s).start()

            @pl.when(has_left)
            def _():
                to_left(0, s).start()

            to_pair(me_b, s).start()

        for h in range(1, depth_z):
            c = s - h
            in_range = jnp.logical_and(c >= 0, c < chunks)

            @pl.when(jnp.logical_and(in_range, z - h >= 0))
            def _():
                from_left(h, c).wait_recv()

                @pl.when(has_right)
                def _():
                    to_right(h, c).start()

                to_pair(me_b - 2 * h, c).start()

            @pl.when(jnp.logical_and(in_range, z + h < depth_z))
            def _():
                from_right(h, c).wait_recv()

                @pl.when(has_left)
                def _():
                    to_left(h, c).start()

                to_pair(me_b + 2 * h, c).start()

        return carry

    lax.fori_loop(0, chunks + depth_z - 1, advance, 0)

    def finish(c, carry):
        for step in range(1, tensors):
            tensor_copy(step, c).wait_send()
        for h in range(depth_z):
            from_pair(h, c).wait_recv()
            to_pair(h * 2 + (me_b % 2), c).wait_send()

            @pl.when(jnp.logical_and(has_right, z - h >= 0))
            def _():
                to_right(h, c).wait_send()

            @pl.when(jnp.logical_and(has_left, z + h < depth_z))
            def _():
                to_left(h, c).wait_send()

        return carry

    lax.fori_loop(0, chunks, finish, 0)


def spread(packed, branches, blk_dev, collective):
    tensors, count, rows, width = packed.shape
    depth_z = branches // 2
    chunk = max(1, count // (8 if depth_z <= 4 else 2))
    while count % chunk:
        chunk -= 1
    chunks = count // chunk
    dma = pltpu.SemaphoreType.DMA
    return pl.pallas_call(
        functools.partial(spread_kernel, branches, tensors, count, chunk),
        out_shape=jax.ShapeDtypeStruct((branches, blk_dev, tensors, rows, width), packed.dtype),
        in_specs=[pl.BlockSpec(memory_space=pltpu.VMEM)],
        out_specs=pl.BlockSpec(memory_space=pl.ANY),
        scratch_shapes=[
            dma((tensors - 1, chunks)),
            dma((tensors - 1, chunks)),
            dma((chunks,)),
        ]
        + [dma((depth_z, chunks))] * 6,
        compiler_params=pltpu.CompilerParams(collective_id=collective, has_side_effects=True),
    )(packed)


def relay_kernel(zs, tensors, blk_dev, region, count, first_cols, width, tab_ref, stored_ref, out_ref,
                 cache_ref, cache_sem, stage, landed, pool_x, in_r, in_l, pool_r, pool_l, ring_r, ring_l,
                 x_send, x_recv, x_own, x_psend, x_precv, x_keep,
                 r_send, r_recv, rp_send, rp_recv, r_keep,
                 l_send, l_recv, lp_send, lp_recv, l_keep):
    me_b = lax.axis_index("branch")
    me_t = lax.axis_index("tensor")
    z = me_b // 2
    core = lax.rem(me_b, 2)
    other = 1 - core
    partner = me_b + 1 - 2 * core
    has_left = z > 0
    has_right = z < zs - 1
    group = 2 * K
    pieces = blk_dev // group
    chunks = count // K
    load = pltpu.make_async_copy(stored_ref, cache_ref, cache_sem)
    load.start()
    barrier = pltpu.get_barrier_semaphore()
    for step in range(1, tensors):
        pl.semaphore_signal(
            barrier, inc=1, device_id={"tensor": lax.rem(me_t + step, tensors)}, device_id_type=MESH
        )
    pl.semaphore_signal(barrier, inc=1, device_id={"branch": partner}, device_id_type=MESH)

    @pl.when(has_left)
    def _():
        pl.semaphore_signal(barrier, inc=1, device_id={"branch": me_b - 2}, device_id_type=MESH)

    @pl.when(has_right)
    def _():
        pl.semaphore_signal(barrier, inc=1, device_id={"branch": me_b + 2}, device_id_type=MESH)

    pl.semaphore_wait(barrier, tensors + jnp.minimum(z, 1) + jnp.minimum(zs - 1 - z, 1))

    def x_span(x):
        return pl.ds(x * group, group)

    def span(c):
        return pl.ds(c * K, K)

    def share(step, x):
        to = lax.rem(me_t + step, tensors)
        return pltpu.make_async_remote_copy(
            src_ref=stage.at[to, x_span(x)],
            dst_ref=landed.at[x_span(x), me_t],
            send_sem=x_send.at[step - 1, x],
            recv_sem=x_recv.at[step - 1, x],
            device_id={"tensor": to},
            device_id_type=MESH,
        )

    def own_part(x):
        return pltpu.make_async_copy(
            stage.at[me_t, x_span(x)], landed.at[x_span(x), me_t], x_own.at[x]
        )

    def x_pair(x):
        return pltpu.make_async_remote_copy(
            src_ref=landed.at[x_span(x)],
            dst_ref=out_ref.at[x_span(x), core],
            send_sem=x_psend.at[x],
            recv_sem=x_precv.at[x],
            device_id={"branch": partner},
            device_id_type=MESH,
        )

    def x_local(x):
        return pltpu.make_async_copy(landed.at[x_span(x)], out_ref.at[x_span(x), core], x_keep.at[x])

    def send(ring, into, target, send_sem, recv_sem, c):
        return pltpu.make_async_remote_copy(
            src_ref=ring.at[span(lax.rem(c, RING))],
            dst_ref=into.at[span(c), core],
            send_sem=send_sem.at[c],
            recv_sem=recv_sem.at[c],
            device_id={"branch": target},
            device_id_type=MESH,
        )

    def pair(into, send_sem, recv_sem, c):
        return pltpu.make_async_remote_copy(
            src_ref=into.at[span(c), core],
            dst_ref=into.at[span(c), core],
            send_sem=send_sem.at[c],
            recv_sem=recv_sem.at[c],
            device_id={"branch": partner},
            device_id_type=MESH,
        )

    def keep(into, base, lane, keep_sem, c):
        return pltpu.make_async_copy(
            into.at[span(c), lane], out_ref.at[pl.ds(base + c * K, K), lane], keep_sem.at[lane, c]
        )

    flows = (
        (1, ring_r, in_r, pool_r, me_b + 2, has_right, has_left, r_send, r_recv, rp_send, rp_recv,
         r_keep, blk_dev),
        (2, ring_l, in_l, pool_l, me_b - 2, has_left, has_right, l_send, l_recv, lp_send, lp_recv,
         l_keep, blk_dev + region),
    )

    def prepare(x):
        def one(j, carry):
            block = tab_ref[0, x * group + j]
            for t, first in enumerate(first_cols):
                stage[t, x * group + j] = cache_ref[block, :, first : first + width]
            return carry

        lax.fori_loop(0, group, one, 0)
        for step in range(1, tensors):
            share(step, x).start()
        own_part(x).start()

    load.wait()
    for x in range(min(LEAD, pieces)):
        prepare(x)

    def advance(s, carry):
        @pl.when(s + LEAD < pieces)
        def _():
            prepare(s + LEAD)

        @pl.when(s < pieces)
        def _():
            for step in range(1, tensors):
                share(step, s).wait_recv()
            own_part(s).wait()
            x_pair(s).start()
            x_local(s).start()

            def one(j, carry):
                pool_x[s * group + j] = landed[s * group + j]
                return carry

            lax.fori_loop(0, group, one, 0)

        for row, ring, into, pool, target, sends, takes, ssem, rsem, pssem, prsem, ksem, base in flows:
            c = s - LAG

            @pl.when(jnp.logical_and(takes, jnp.logical_and(c >= 0, c < chunks)))
            def _():
                pair(into, pssem, prsem, c).wait_recv()
                keep(into, base, other, ksem, c).start()

                def one(j, carry):
                    pool[2 * (c * K + j)] = into[c * K + j, 0]
                    pool[2 * (c * K + j) + 1] = into[c * K + j, 1]
                    return carry

                lax.fori_loop(0, K, one, 0)

        for row, ring, into, pool, target, sends, takes, ssem, rsem, pssem, prsem, ksem, base in flows:

            @pl.when(jnp.logical_and(sends, s < chunks))
            def _():
                @pl.when(s >= RING)
                def _():
                    send(ring, into, target, ssem, rsem, s - RING).wait_send()

                def one(j, carry):
                    source = tab_ref[row, s * K + j]
                    near = pool_x[jnp.minimum(source, blk_dev - 1)]
                    far = pool[jnp.clip(source - blk_dev, 0, 2 * count - 1)]
                    ring[lax.rem(s, RING) * K + j] = jnp.where(source < blk_dev, near, far)
                    return carry

                lax.fori_loop(0, K, one, 0)
                send(ring, into, target, ssem, rsem, s).start()

        for row, ring, into, pool, target, sends, takes, ssem, rsem, pssem, prsem, ksem, base in flows:
            c = s - ARRIVE

            @pl.when(jnp.logical_and(takes, jnp.logical_and(c >= 0, c < chunks)))
            def _():
                send(ring, into, me_b, ssem, rsem, c).wait_recv()
                pair(into, pssem, prsem, c).start()
                keep(into, base, core, ksem, c).start()

        return carry

    lax.fori_loop(0, max(chunks + LAG, pieces), advance, 0)

    def finish_x(x, carry):
        for step in range(1, tensors):
            share(step, x).wait_send()
        x_pair(x).wait()
        x_local(x).wait()
        return carry

    lax.fori_loop(0, pieces, finish_x, 0)

    def finish(c, carry):
        for row, ring, into, pool, target, sends, takes, ssem, rsem, pssem, prsem, ksem, base in flows:

            @pl.when(takes)
            def _():
                pair(into, pssem, prsem, c).wait_send()
                keep(into, base, 0, ksem, c).wait()
                keep(into, base, 1, ksem, c).wait()

            @pl.when(jnp.logical_and(sends, c >= chunks - RING))
            def _():
                send(ring, into, target, ssem, rsem, c).wait_send()

        return carry

    lax.fori_loop(0, chunks, finish, 0)


def relay(table, cache, zs, tensors, count, region, first_cols, width, collective):
    blk_dev, rows, _ = cache.shape
    total = 2 * zs * blk_dev
    dma = pltpu.SemaphoreType.DMA
    pieces = blk_dev // (2 * K)
    chunks = count // K
    block = (tensors, rows, width)
    flow = [dma((chunks,))] * 4 + [dma((2, chunks))]
    return pl.pallas_call(
        functools.partial(
            relay_kernel, zs, tensors, blk_dev, region, count, first_cols, width
        ),
        out_shape=jax.ShapeDtypeStruct((total // 2, 2) + block, cache.dtype),
        in_specs=[pl.BlockSpec(memory_space=pltpu.SMEM), pl.BlockSpec(memory_space=pl.ANY)],
        out_specs=pl.BlockSpec(memory_space=pl.ANY),
        scratch_shapes=[
            pltpu.VMEM(cache.shape, cache.dtype),
            dma,
            pltpu.VMEM((tensors, blk_dev, rows, width), cache.dtype),
            pltpu.VMEM((blk_dev,) + block, cache.dtype),
            pltpu.VMEM((blk_dev,) + block, cache.dtype),
            pltpu.VMEM((count, 2) + block, cache.dtype),
            pltpu.VMEM((count, 2) + block, cache.dtype),
            pltpu.VMEM((2 * count,) + block, cache.dtype),
            pltpu.VMEM((2 * count,) + block, cache.dtype),
            pltpu.VMEM((RING * K,) + block, cache.dtype),
            pltpu.VMEM((RING * K,) + block, cache.dtype),
            dma((tensors - 1, pieces)),
            dma((tensors - 1, pieces)),
        ]
        + [dma((pieces,))] * 4
        + flow
        + flow,
        compiler_params=pltpu.CompilerParams(
            collective_id=collective, has_side_effects=True, vmem_limit_bytes=62 * 2**20
        ),
    )(table, cache)


def attend_kernel(nodes, kv_dev, group_q, tab_ref, q_ref, fresh_ref, *refs):
    kv_refs = refs[:STEP_BLOCKS]
    out_ref, q_s, m_s, l_s, acc_s = refs[STEP_BLOCKS:]
    i = pl.program_id(0)
    factor = math.log2(math.e) / math.sqrt(HD)
    rows = group_q * NODE_TOK
    tile = min(rows, 256)
    contract = (((1,), (1,)), ((), ()))

    @pl.when(i == 0)
    def _():
        row = lax.broadcasted_iota(jnp.int32, (tile, NODE_TOK), 0) & (NODE_TOK - 1)
        col = lax.broadcasted_iota(jnp.int32, (tile, NODE_TOK), 1)
        causal = col <= row
        for n in range(nodes):
            tok = slice(n * NODE_TOK, (n + 1) * NODE_TOK)
            for h in range(kv_dev):
                k = fresh_ref[tok, h * 2 * HD : h * 2 * HD + HD]
                v = fresh_ref[tok, h * 2 * HD + HD : (h + 1) * 2 * HD]
                kk = jnp.concatenate([k, k], axis=1)
                vv = jnp.concatenate([v, jnp.ones_like(v)], axis=1)
                p = n * kv_dev + h
                for a in range(group_q):
                    head = h * group_q + a
                    here = slice(a * NODE_TOK, (a + 1) * NODE_TOK)
                    wide_q = q_ref[tok, head * HD : (head + 1) * HD].astype(jnp.float32) * factor
                    upper = wide_q.astype(jnp.bfloat16)
                    q_s[p, here, :HD] = upper
                    q_s[p, here, HD:] = (wide_q - upper.astype(jnp.float32)).astype(jnp.bfloat16)
                for start in range(0, rows, tile):
                    here = slice(start, start + tile)
                    s = lax.dot_general(
                        q_s[p, here, :], kk, contract, preferred_element_type=jnp.float32
                    )
                    s = jnp.where(causal, s, -jnp.inf)
                    m = jnp.max(s, axis=1, keepdims=True)
                    w = jnp.exp2(s - m)
                    m_s[p, here, :] = jnp.broadcast_to(m, (tile, 128))
                    both = jnp.dot(w.astype(jnp.bfloat16), vv, preferred_element_type=jnp.float32)
                    acc_s[p, here, :] = both[:, :HD]
                    l_s[p, here, :] = both[:, HD:]

    def visit(n, masked):
        keys = STEP_BLOCKS * BT
        if masked:
            slot = lax.broadcasted_iota(jnp.int32, (1, keys), 1) // BT + i * STEP_BLOCKS
            seen = slot < tab_ref[5, n]
        for h in range(kv_dev):
            k = jnp.concatenate([r[0, :, h * 2 * HD : h * 2 * HD + HD] for r in kv_refs], axis=0)
            v = jnp.concatenate([r[0, :, h * 2 * HD + HD : (h + 1) * 2 * HD] for r in kv_refs], axis=0)
            vv = jnp.concatenate([v, jnp.ones_like(v)], axis=1)
            kk = jnp.concatenate([k, k], axis=1)
            p = n * kv_dev + h
            for start in range(0, rows, tile):
                here = slice(start, start + tile)
                s = lax.dot_general(
                    q_s[p, here, :], kk, contract, preferred_element_type=jnp.float32
                )
                if masked:
                    s = jnp.where(seen, s, -jnp.inf)
                m_old = m_s[p, here, :]
                m_new = jnp.maximum(m_old, jnp.max(s, axis=1, keepdims=True))
                alpha = jnp.exp2(m_old - m_new)
                w = [jnp.exp2(s[:, u * 128 : (u + 1) * 128] - m_new) for u in range(keys // 128)]
                wide = jnp.concatenate([x.astype(jnp.bfloat16) for x in w], axis=1)
                both = jnp.dot(wide, vv, preferred_element_type=jnp.float32)
                acc_s[p, here, :] = acc_s[p, here, :] * alpha + both[:, :HD]
                l_s[p, here, :] = l_s[p, here, :] * alpha + both[:, HD:]
                m_s[p, here, :] = m_new

    for n in range(nodes):
        first = i * STEP_BLOCKS
        whole = first + STEP_BLOCKS <= tab_ref[5, n]

        @pl.when(whole)
        def _():
            visit(n, False)

        @pl.when(jnp.logical_and(first < tab_ref[5, n], jnp.logical_not(whole)))
        def _():
            visit(n, True)

    @pl.when(i == pl.num_programs(0) - 1)
    def _():
        for n in range(nodes):
            for h in range(kv_dev):
                p = n * kv_dev + h
                for a in range(group_q):
                    head = h * group_q + a
                    here = slice(a * NODE_TOK, (a + 1) * NODE_TOK)
                    total = l_s[p, here, :]
                    out_ref[n * NODE_TOK : (n + 1) * NODE_TOK, head * HD : (head + 1) * HD] = (
                        acc_s[p, here, :] / total
                    ).astype(out_ref.dtype)


def attend(queries, fresh, blocks, table, nodes, kv_dev, group_q):
    new_rows, q_cols = queries.shape
    width = blocks.shape[2]
    rows = group_q * NODE_TOK
    pairs = nodes * kv_dev

    def kv_spec(u):
        return pl.BlockSpec((1, BT, width), lambda i, tab: (tab[3, i * STEP_BLOCKS + u], 0, 0))

    return pl.pallas_call(
        functools.partial(attend_kernel, nodes, kv_dev, group_q),
        out_shape=jax.ShapeDtypeStruct((new_rows, q_cols), queries.dtype),
        grid_spec=pltpu.PrefetchScalarGridSpec(
            num_scalar_prefetch=1,
            grid=(P_SIZE // STEP_BLOCKS,),
            in_specs=[
                pl.BlockSpec((new_rows, q_cols), lambda i, tab: (0, 0)),
                pl.BlockSpec((new_rows, width), lambda i, tab: (0, 0)),
            ]
            + [kv_spec(u) for u in range(STEP_BLOCKS)],
            out_specs=pl.BlockSpec((new_rows, q_cols), lambda i, tab: (0, 0)),
            scratch_shapes=[
                pltpu.VMEM((pairs, rows, 2 * HD), jnp.bfloat16),
                pltpu.VMEM((pairs, rows, 128), jnp.float32),
                pltpu.VMEM((pairs, rows, 128), jnp.float32),
                pltpu.VMEM((pairs, rows, HD), jnp.float32),
            ],
        ),
        compiler_params=pltpu.CompilerParams(vmem_limit_bytes=48 * 2**20),
    )(table, queries, fresh, *([blocks] * STEP_BLOCKS))


def body(queries, new_kv, cache, parents, depth):
    tensor_size = lax.axis_size("tensor")
    branches = lax.axis_size("branch")
    tensor_pos = lax.axis_index("tensor")
    branch_pos = lax.axis_index("branch")
    sharing = HQ // KVH
    heads_dev = queries.shape[1] // HD
    kv_dev = max(1, heads_dev // sharing)
    group_q = heads_dev // kv_dev
    first_kv = tensor_pos * heads_dev // sharing
    blk_dev = cache.shape[0]
    new_rows = queries.shape[0]
    width = kv_dev * 2 * HD
    nodes = depth.shape[1]
    zs = branches // 2
    first_cols = [(t * heads_dev // sharing) * 2 * HD for t in range(tensor_size)]
    fresh = lax.dynamic_slice_in_dim(new_kv, first_kv, kv_dev, 1).reshape(new_rows, width)
    out_blocks = (branches * blk_dev // 2, 2, tensor_size, cache.shape[1], width)

    def flood(cache, picks, collective):
        packed = pack(cache, picks, blk_dev, first_cols, width)
        return spread(packed, branches, blk_dev, collective).reshape(out_blocks)

    region = (branches * blk_dev - 2 * blk_dev) // 4
    every = jnp.arange(blk_dev, dtype=jnp.int32)
    if zs <= 4 and blk_dev % (2 * K) == 0 and region >= LEVELS[-1] and branches * blk_dev <= 256:
        table = make_plan(parents, depth, branches, blk_dev, region)

        def with_count(count, collective):
            def run(table, cache):
                return relay(
                    table, cache, zs, tensor_size, count, region, first_cols, width, collective
                )

            return run

        runs = [with_count(count, 1 + i) for i, count in enumerate(LEVELS)]
        runs.append(lambda table, cache: flood(cache, every, 1 + len(LEVELS)))
        gathered = lax.switch(table[4, 0], runs, table, cache)
    else:
        own_row = lax.dynamic_index_in_dim(parents, branch_pos, 0, keepdims=False)
        own_row = own_row[jnp.minimum(jnp.arange(P_SIZE), jnp.max(depth[0]) - 1)]
        filler = jnp.zeros((128,), jnp.int32)
        rows = [filler] * 3 + [filler.at[:P_SIZE].set(own_row), filler, filler.at[:nodes].set(depth[0])]
        table = jnp.stack(rows + [filler] * 2)
        gathered = flood(cache, every, 1)
    blocks = gathered.reshape(branches * blk_dev, BT, width)
    return attend(queries, fresh, blocks, table, nodes, kv_dev, group_q)


def solution(mesh):
    placed = (
        P("branch", "tensor"),
        P("branch", None, None),
        P("branch", "tensor", None),
        P(),
        P("branch", None),
    )
    return jax.shard_map(
        body, mesh=mesh, in_specs=placed, out_specs=P("branch", "tensor"), check_vma=False
    )
```

```python
import functools
import math

import jax
import jax.numpy as jnp
from jax import lax
from jax.experimental import pallas as pl
from jax.experimental.pallas import tpu as pltpu
from jax.sharding import PartitionSpec as P

HQ = 64
KVH = 8
HD = 128
BT = 128
NODE_TOK = 128
P_SIZE = 48
STEP_BLOCKS = 8
K = 1
LAG = 4
ARRIVE = 2
RING = 6
LEAD = 6
LEVELS = (22, 24, 26, 28, 30, 32, 35, 42)
MESH = pl.DeviceIdType.MESH


def plan(zs, blk_dev, region, levels, parents, deep, me):
    n = 2 * zs
    nb = n * blk_dev
    big = 1 << 20
    i32 = jnp.int32
    listed = parents.shape[1]
    lane = lax.broadcasted_iota(i32, (n, listed), 1)
    act = jnp.where(lane < deep, parents, -1)
    blk = lax.broadcasted_iota(i32, (nb, listed), 0)
    need = []
    for z in range(zs):
        hit = (act[2 * z : 2 * z + 1, :] == blk) | (act[2 * z + 1 : 2 * z + 2, :] == blk)
        need.append(jnp.max(jnp.where(hit, 1, 0), axis=1, keepdims=True) > 0)
    bcol = lax.broadcasted_iota(i32, (nb, 1), 0)
    owner = jnp.zeros((nb, 1), i32)
    for o in range(1, n):
        owner = owner + jnp.where(bcol >= o * blk_dev, 1, 0)
    zb = owner >> 1
    cb = owner & 1
    eye = lax.broadcasted_iota(i32, (nb, nb), 0) == lax.broadcasted_iota(i32, (nb, nb), 1)

    def row(x):
        return jnp.sum(jnp.where(eye, x, 0), axis=0, keepdims=True)

    def rank(key):
        return jnp.sum(jnp.where(row(key) < key, 1, 0), axis=1, keepdims=True)

    def direction(fwd):
        zc = zb if fwd else zs - 1 - zb
        far = jnp.full((nb, 1), -1, i32)
        for z in range(zs):
            zz = z if fwd else zs - 1 - z
            far = jnp.where(need[z] & (zz > zc), jnp.maximum(far, zz), far)
        own_rank = jnp.full((nb, 1), big, i32)
        slots = []
        total = jnp.zeros((1, 1), i32)
        prev = jnp.zeros((nb, 1), i32)
        for k in range(zs - 1):
            own = (zc == k) & (far > k)
            rel = (zc < k) & (far > k)
            first = (cb * zs + (zs - far)) * nb + bcol
            key = jnp.where(own, first, jnp.where(rel, big + prev, 2 * big + bcol))
            key_row = row(key)
            r0 = jnp.sum(jnp.where(key_row < key, 1, 0), axis=1, keepdims=True)
            n0 = jnp.sum(jnp.where(own & (cb == 0), 1, 0), axis=0, keepdims=True)
            n1 = jnp.sum(jnp.where(own & (cb == 1), 1, 0), axis=0, keepdims=True)
            top = jnp.maximum(n0, n1)
            short = jnp.where(n0 <= n1, 0, 1)
            mine = r0 - cb * n0
            if k > 0:
                ready = (prev >> (K.bit_length())) + LAG
                at = jnp.where(ready * K <= top, top + ready * K, 2 * K * ready)
                gap_row = row(jnp.where(rel, at - r0, -big))
                gap = jnp.max(jnp.where(key_row <= key, gap_row, -big), axis=1, keepdims=True)
                r = r0 + jnp.maximum(gap, 0)
            else:
                r = r0
            far_slot = jnp.where(r < 2 * top, 2 * (r - top) + short, r)
            q = jnp.where(own, 2 * mine + cb, jnp.where(rel, far_slot, -1))
            own_rank = jnp.where(own, mine, own_rank)
            total = jnp.maximum(total, jnp.max(q, axis=0, keepdims=True) + 1)
            slots.append(q)
            prev = jnp.maximum(q, 0)
        return slots, own_rank, total

    right, rank_r, total_r = direction(True)
    left, rank_l, total_l = direction(False)
    local = jnp.zeros((nb, 1), jnp.bool_)
    for z in range(zs):
        local = local | (need[z] & (zb == z))
    key = jnp.minimum(2 * rank_r, 2 * rank_l + 1)
    key = jnp.where(key < big, key, jnp.where(local, big // 2 + bcol, big + bcol))
    order = rank(owner * (4 * big) + key) - owner * blk_dev

    me_z = me // 2
    me_c = me % 2
    lanes = lax.broadcasted_iota(i32, (1, 128), 1)

    def table(where_col, value_col):
        return jnp.sum(jnp.where(where_col == lanes, value_col, 0), axis=0, keepdims=True)

    def pick_link(slots, k):
        q = jnp.full((nb, 1), -1, i32)
        for j in range(zs - 1):
            q = jnp.where(k == j, slots[j], q)
        return q

    mine = owner == me
    picks = table(jnp.where(mine, order, -1), bcol - owner * blk_dev)

    def sources(slots, k):
        q = pick_link(slots, k)
        came = pick_link(slots, k - 1)
        source = jnp.where(zb == me_z, order, blk_dev + came)
        use = (q >= 0) & ((q & 1) == me_c)
        return table(jnp.where(use, q >> 1, -1), source)

    sel_r = sources(right, me_z)
    sel_l = sources(left, zs - 1 - me_z)
    from_r = pick_link(right, me_z - 1)
    from_l = pick_link(left, zs - 2 - me_z)
    place = jnp.where(
        zb == me_z,
        2 * order + cb,
        jnp.where(zb < me_z, 2 * blk_dev + from_r, 2 * (blk_dev + region) + from_l),
    )
    slot_count = (jnp.maximum(total_r, total_l) + 1) >> 1
    choice = jnp.zeros((1, 1), i32)
    for c in levels:
        choice = choice + jnp.where(slot_count > c, 1, 0)
    place = jnp.where(choice == len(levels), bcol, place)
    groups = lax.broadcasted_iota(i32, (n, listed), 0)
    my_row = jnp.sum(jnp.where(groups == me, act, 0), axis=0, keepdims=True)
    last = jnp.sum(jnp.where((groups == me) & (lane == deep - 1), act, 0), axis=(0, 1), keepdims=True)
    my_row = jnp.where(my_row < 0, last, my_row)
    pos = jnp.sum(jnp.where(bcol == my_row, place, 0), axis=0, keepdims=True)
    return picks, sel_r, sel_l, pos, choice, slot_count


def plan_kernel(zs, blk_dev, region, parents_ref, mine_ref, table_ref, all_ref, send_sem, recv_sem):
    n = 2 * zs
    me = lax.axis_index("branch")
    barrier = pltpu.get_barrier_semaphore()

    def greet(i, carry):
        peer = lax.rem(me + i, n)
        pl.semaphore_signal(barrier, inc=1, device_id={"branch": peer}, device_id_type=MESH)
        return carry

    lax.fori_loop(1, n, greet, 0)
    pl.semaphore_wait(barrier, n - 1)

    def copy(i):
        return pltpu.make_async_remote_copy(
            src_ref=mine_ref,
            dst_ref=all_ref.at[me],
            send_sem=send_sem.at[i],
            recv_sem=recv_sem.at[i],
            device_id={"branch": lax.rem(me + i, n)},
            device_id_type=MESH,
        )

    def start(i, carry):
        copy(i).start()
        return carry

    def finish(i, carry):
        copy(i).wait()
        return carry

    lax.fori_loop(1, n, start, 0)
    all_ref[pl.ds(me, 1)] = mine_ref[...][None]
    lax.fori_loop(1, n, finish, 0)
    deep = jnp.concatenate([jnp.max(all_ref[g, 0:1, :], axis=1, keepdims=True) for g in range(n)], axis=0)
    picks, sel_r, sel_l, pos, choice, _ = plan(
        zs, blk_dev, region, LEVELS, parents_ref[...], deep, me
    )
    table_ref[0:1, :] = picks
    table_ref[1:2, :] = sel_r
    table_ref[2:3, :] = sel_l
    table_ref[3:4, 0 : pos.shape[1]] = pos
    table_ref[4:5, :] = jnp.broadcast_to(choice, (1, 128))
    table_ref[5:6, :] = mine_ref[0:1, :]


def make_plan(parents, depth, n, blk_dev, region):
    nodes = depth.shape[1]
    mine = jnp.pad(depth, ((0, 7), (0, 128 - nodes)))
    return pl.pallas_call(
        functools.partial(plan_kernel, n // 2, blk_dev, region),
        out_shape=jax.ShapeDtypeStruct((8, 128), jnp.int32),
        in_specs=[pl.BlockSpec(memory_space=pltpu.VMEM)] * 2,
        out_specs=pl.BlockSpec(memory_space=pltpu.VMEM),
        scratch_shapes=[
            pltpu.VMEM((n, 8, 128), jnp.int32),
            pltpu.SemaphoreType.DMA((n,)),
            pltpu.SemaphoreType.DMA((n,)),
        ],
        compiler_params=pltpu.CompilerParams(collective_id=0, has_side_effects=True),
    )(parents, mine)


def pack_kernel(first_cols, width, pick_ref, block_ref, packed_ref):
    for t, first in enumerate(first_cols):
        packed_ref[t, 0] = block_ref[0, :, first : first + width]


def pack(cache, picks, count, first_cols, width):
    rows = cache.shape[1]
    tensors = len(first_cols)
    return pl.pallas_call(
        functools.partial(pack_kernel, first_cols, width),
        out_shape=jax.ShapeDtypeStruct((tensors, count, rows, width), cache.dtype),
        grid_spec=pltpu.PrefetchScalarGridSpec(
            num_scalar_prefetch=1,
            grid=(count,),
            in_specs=[pl.BlockSpec((1, rows, cache.shape[2]), lambda i, pick: (pick[i], 0, 0))],
            out_specs=pl.BlockSpec((tensors, 1, rows, width), lambda i, pick: (0, i, 0, 0)),
        ),
    )(picks, cache)


def spread_kernel(branches, tensors, count, chunk, packed_ref, out_ref, tp_send, tp_recv, own_sem,
                  right_send, right_recv, left_send, left_recv, pair_send, pair_recv):
    me_b = lax.axis_index("branch")
    me_t = lax.axis_index("tensor")
    z = me_b // 2
    depth_z = branches // 2
    partner = me_b + 1 - 2 * (me_b % 2)
    chunks = count // chunk
    has_left = z > 0
    has_right = z < depth_z - 1
    barrier = pltpu.get_barrier_semaphore()
    for step in range(1, tensors):
        pl.semaphore_signal(
            barrier, inc=1, device_id={"tensor": lax.rem(me_t + step, tensors)}, device_id_type=MESH
        )
    pl.semaphore_signal(barrier, inc=1, device_id={"branch": partner}, device_id_type=MESH)

    @pl.when(has_left)
    def _():
        pl.semaphore_signal(barrier, inc=1, device_id={"branch": me_b - 2}, device_id_type=MESH)

    @pl.when(has_right)
    def _():
        pl.semaphore_signal(barrier, inc=1, device_id={"branch": me_b + 2}, device_id_type=MESH)

    pl.semaphore_wait(barrier, tensors + jnp.minimum(z, 1) + jnp.minimum(depth_z - 1 - z, 1))

    def span(c):
        return pl.ds(c * chunk, chunk)

    def tensor_copy(step, c):
        to = lax.rem(me_t + step, tensors)
        return pltpu.make_async_remote_copy(
            src_ref=packed_ref.at[to, span(c)],
            dst_ref=out_ref.at[me_b, span(c), me_t],
            send_sem=tp_send.at[step - 1, c],
            recv_sem=tp_recv.at[step - 1, c],
            device_id={"tensor": to},
            device_id_type=MESH,
        )

    def own_copy(c):
        return pltpu.make_async_copy(
            packed_ref.at[me_t, span(c)], out_ref.at[me_b, span(c), me_t], own_sem.at[c]
        )

    def lane_copy(origin, c, target, send_sem, recv_sem):
        return pltpu.make_async_remote_copy(
            src_ref=out_ref.at[origin, span(c)],
            dst_ref=out_ref.at[origin, span(c)],
            send_sem=send_sem,
            recv_sem=recv_sem,
            device_id={"branch": target},
            device_id_type=MESH,
        )

    def to_right(h, c):
        return lane_copy(me_b - 2 * h, c, me_b + 2, right_send.at[h, c], right_recv.at[h + 1, c])

    def from_left(h, c):
        return lane_copy(me_b - 2 * h, c, me_b, right_send.at[h, c], right_recv.at[h, c])

    def to_left(h, c):
        return lane_copy(me_b + 2 * h, c, me_b - 2, left_send.at[h, c], left_recv.at[h + 1, c])

    def from_right(h, c):
        return lane_copy(me_b + 2 * h, c, me_b, left_send.at[h, c], left_recv.at[h, c])

    def to_pair(origin, c):
        return lane_copy(origin, c, partner, pair_send.at[origin // 2, c], pair_recv.at[origin // 2, c])

    def from_pair(origin_z, c):
        origin = origin_z * 2 + 1 - (me_b % 2)
        return lane_copy(origin, c, partner, pair_send.at[origin_z, c], pair_recv.at[origin_z, c])

    def start_tensor(c, carry):
        own_copy(c).start()
        for step in range(1, tensors):
            tensor_copy(step, c).start()
        return carry

    lax.fori_loop(0, chunks, start_tensor, 0)

    def advance(s, carry):
        @pl.when(s < chunks)
        def _():
            for step in range(1, tensors):
                tensor_copy(step, s).wait_recv()
            own_copy(s).wait()

            @pl.when(has_right)
            def _():
                to_right(0, s).start()

            @pl.when(has_left)
            def _():
                to_left(0, s).start()

            to_pair(me_b, s).start()

        for h in range(1, depth_z):
            c = s - h
            in_range = jnp.logical_and(c >= 0, c < chunks)

            @pl.when(jnp.logical_and(in_range, z - h >= 0))
            def _():
                from_left(h, c).wait_recv()

                @pl.when(has_right)
                def _():
                    to_right(h, c).start()

                to_pair(me_b - 2 * h, c).start()

            @pl.when(jnp.logical_and(in_range, z + h < depth_z))
            def _():
                from_right(h, c).wait_recv()

                @pl.when(has_left)
                def _():
                    to_left(h, c).start()

                to_pair(me_b + 2 * h, c).start()

        return carry

    lax.fori_loop(0, chunks + depth_z - 1, advance, 0)

    def finish(c, carry):
        for step in range(1, tensors):
            tensor_copy(step, c).wait_send()
        for h in range(depth_z):
            from_pair(h, c).wait_recv()
            to_pair(h * 2 + (me_b % 2), c).wait_send()

            @pl.when(jnp.logical_and(has_right, z - h >= 0))
            def _():
                to_right(h, c).wait_send()

            @pl.when(jnp.logical_and(has_left, z + h < depth_z))
            def _():
                to_left(h, c).wait_send()

        return carry

    lax.fori_loop(0, chunks, finish, 0)


def spread(packed, branches, blk_dev, collective):
    tensors, count, rows, width = packed.shape
    depth_z = branches // 2
    chunk = max(1, count // (8 if depth_z <= 4 else 2))
    while count % chunk:
        chunk -= 1
    chunks = count // chunk
    dma = pltpu.SemaphoreType.DMA
    return pl.pallas_call(
        functools.partial(spread_kernel, branches, tensors, count, chunk),
        out_shape=jax.ShapeDtypeStruct((branches, blk_dev, tensors, rows, width), packed.dtype),
        in_specs=[pl.BlockSpec(memory_space=pltpu.VMEM)],
        out_specs=pl.BlockSpec(memory_space=pl.ANY),
        scratch_shapes=[
            dma((tensors - 1, chunks)),
            dma((tensors - 1, chunks)),
            dma((chunks,)),
        ]
        + [dma((depth_z, chunks))] * 6,
        compiler_params=pltpu.CompilerParams(collective_id=collective, has_side_effects=True),
    )(packed)


def relay_kernel(zs, tensors, blk_dev, region, count, first_cols, width, tab_ref, stored_ref, out_ref,
                 cache_ref, cache_sem, stage, landed, pool_x, in_r, in_l, pool_r, pool_l, ring_r, ring_l,
                 x_send, x_recv, x_own, x_psend, x_precv, x_keep,
                 r_send, r_recv, rp_send, rp_recv, r_keep,
                 l_send, l_recv, lp_send, lp_recv, l_keep):
    me_b = lax.axis_index("branch")
    me_t = lax.axis_index("tensor")
    z = me_b // 2
    core = lax.rem(me_b, 2)
    other = 1 - core
    partner = me_b + 1 - 2 * core
    has_left = z > 0
    has_right = z < zs - 1
    group = 2 * K
    pieces = blk_dev // group
    chunks = count // K
    load = pltpu.make_async_copy(stored_ref, cache_ref, cache_sem)
    load.start()
    barrier = pltpu.get_barrier_semaphore()
    for step in range(1, tensors):
        pl.semaphore_signal(
            barrier, inc=1, device_id={"tensor": lax.rem(me_t + step, tensors)}, device_id_type=MESH
        )
    pl.semaphore_signal(barrier, inc=1, device_id={"branch": partner}, device_id_type=MESH)

    @pl.when(has_left)
    def _():
        pl.semaphore_signal(barrier, inc=1, device_id={"branch": me_b - 2}, device_id_type=MESH)

    @pl.when(has_right)
    def _():
        pl.semaphore_signal(barrier, inc=1, device_id={"branch": me_b + 2}, device_id_type=MESH)

    pl.semaphore_wait(barrier, tensors + jnp.minimum(z, 1) + jnp.minimum(zs - 1 - z, 1))

    def x_span(x):
        return pl.ds(x * group, group)

    def span(c):
        return pl.ds(c * K, K)

    def share(step, x):
        to = lax.rem(me_t + step, tensors)
        return pltpu.make_async_remote_copy(
            src_ref=stage.at[to, x_span(x)],
            dst_ref=landed.at[x_span(x), me_t],
            send_sem=x_send.at[step - 1, x],
            recv_sem=x_recv.at[step - 1, x],
            device_id={"tensor": to},
            device_id_type=MESH,
        )

    def own_part(x):
        return pltpu.make_async_copy(
            stage.at[me_t, x_span(x)], landed.at[x_span(x), me_t], x_own.at[x]
        )

    def x_pair(x):
        return pltpu.make_async_remote_copy(
            src_ref=landed.at[x_span(x)],
            dst_ref=out_ref.at[x_span(x), core],
            send_sem=x_psend.at[x],
            recv_sem=x_precv.at[x],
            device_id={"branch": partner},
            device_id_type=MESH,
        )

    def x_local(x):
        return pltpu.make_async_copy(landed.at[x_span(x)], out_ref.at[x_span(x), core], x_keep.at[x])

    def send(ring, into, target, send_sem, recv_sem, c):
        return pltpu.make_async_remote_copy(
            src_ref=ring.at[span(lax.rem(c, RING))],
            dst_ref=into.at[span(c), core],
            send_sem=send_sem.at[c],
            recv_sem=recv_sem.at[c],
            device_id={"branch": target},
            device_id_type=MESH,
        )

    def pair(into, send_sem, recv_sem, c):
        return pltpu.make_async_remote_copy(
            src_ref=into.at[span(c), core],
            dst_ref=into.at[span(c), core],
            send_sem=send_sem.at[c],
            recv_sem=recv_sem.at[c],
            device_id={"branch": partner},
            device_id_type=MESH,
        )

    def keep(into, base, lane, keep_sem, c):
        return pltpu.make_async_copy(
            into.at[span(c), lane], out_ref.at[pl.ds(base + c * K, K), lane], keep_sem.at[lane, c]
        )

    flows = (
        (1, ring_r, in_r, pool_r, me_b + 2, has_right, has_left, r_send, r_recv, rp_send, rp_recv,
         r_keep, blk_dev),
        (2, ring_l, in_l, pool_l, me_b - 2, has_left, has_right, l_send, l_recv, lp_send, lp_recv,
         l_keep, blk_dev + region),
    )

    def prepare(x):
        def one(j, carry):
            block = tab_ref[0, x * group + j]
            for t, first in enumerate(first_cols):
                stage[t, x * group + j] = cache_ref[block, :, first : first + width]
            return carry

        lax.fori_loop(0, group, one, 0)
        for step in range(1, tensors):
            share(step, x).start()
        own_part(x).start()

    load.wait()
    for x in range(min(LEAD, pieces)):
        prepare(x)

    def advance(s, carry):
        @pl.when(s + LEAD < pieces)
        def _():
            prepare(s + LEAD)

        @pl.when(s < pieces)
        def _():
            for step in range(1, tensors):
                share(step, s).wait_recv()
            own_part(s).wait()
            x_pair(s).start()
            x_local(s).start()

            def one(j, carry):
                pool_x[s * group + j] = landed[s * group + j]
                return carry

            lax.fori_loop(0, group, one, 0)

        for row, ring, into, pool, target, sends, takes, ssem, rsem, pssem, prsem, ksem, base in flows:
            c = s - LAG

            @pl.when(jnp.logical_and(takes, jnp.logical_and(c >= 0, c < chunks)))
            def _():
                pair(into, pssem, prsem, c).wait_recv()
                keep(into, base, other, ksem, c).start()

                def one(j, carry):
                    pool[2 * (c * K + j)] = into[c * K + j, 0]
                    pool[2 * (c * K + j) + 1] = into[c * K + j, 1]
                    return carry

                lax.fori_loop(0, K, one, 0)

        for row, ring, into, pool, target, sends, takes, ssem, rsem, pssem, prsem, ksem, base in flows:

            @pl.when(jnp.logical_and(sends, s < chunks))
            def _():
                @pl.when(s >= RING)
                def _():
                    send(ring, into, target, ssem, rsem, s - RING).wait_send()

                def one(j, carry):
                    source = tab_ref[row, s * K + j]
                    near = pool_x[jnp.minimum(source, blk_dev - 1)]
                    far = pool[jnp.clip(source - blk_dev, 0, 2 * count - 1)]
                    ring[lax.rem(s, RING) * K + j] = jnp.where(source < blk_dev, near, far)
                    return carry

                lax.fori_loop(0, K, one, 0)
                send(ring, into, target, ssem, rsem, s).start()

        for row, ring, into, pool, target, sends, takes, ssem, rsem, pssem, prsem, ksem, base in flows:
            c = s - ARRIVE

            @pl.when(jnp.logical_and(takes, jnp.logical_and(c >= 0, c < chunks)))
            def _():
                send(ring, into, me_b, ssem, rsem, c).wait_recv()
                pair(into, pssem, prsem, c).start()
                keep(into, base, core, ksem, c).start()

        return carry

    lax.fori_loop(0, max(chunks + LAG, pieces), advance, 0)

    def finish_x(x, carry):
        for step in range(1, tensors):
            share(step, x).wait_send()
        x_pair(x).wait()
        x_local(x).wait()
        return carry

    lax.fori_loop(0, pieces, finish_x, 0)

    def finish(c, carry):
        for row, ring, into, pool, target, sends, takes, ssem, rsem, pssem, prsem, ksem, base in flows:

            @pl.when(takes)
            def _():
                pair(into, pssem, prsem, c).wait_send()
                keep(into, base, 0, ksem, c).wait()
                keep(into, base, 1, ksem, c).wait()

            @pl.when(jnp.logical_and(sends, c >= chunks - RING))
            def _():
                send(ring, into, target, ssem, rsem, c).wait_send()

        return carry

    lax.fori_loop(0, chunks, finish, 0)


def relay(table, cache, zs, tensors, count, region, first_cols, width, collective):
    blk_dev, rows, _ = cache.shape
    total = 2 * zs * blk_dev
    dma = pltpu.SemaphoreType.DMA
    pieces = blk_dev // (2 * K)
    chunks = count // K
    block = (tensors, rows, width)
    flow = [dma((chunks,))] * 4 + [dma((2, chunks))]
    return pl.pallas_call(
        functools.partial(
            relay_kernel, zs, tensors, blk_dev, region, count, first_cols, width
        ),
        out_shape=jax.ShapeDtypeStruct((total // 2, 2) + block, cache.dtype),
        in_specs=[pl.BlockSpec(memory_space=pltpu.SMEM), pl.BlockSpec(memory_space=pl.ANY)],
        out_specs=pl.BlockSpec(memory_space=pl.ANY),
        scratch_shapes=[
            pltpu.VMEM(cache.shape, cache.dtype),
            dma,
            pltpu.VMEM((tensors, blk_dev, rows, width), cache.dtype),
            pltpu.VMEM((blk_dev,) + block, cache.dtype),
            pltpu.VMEM((blk_dev,) + block, cache.dtype),
            pltpu.VMEM((count, 2) + block, cache.dtype),
            pltpu.VMEM((count, 2) + block, cache.dtype),
            pltpu.VMEM((2 * count,) + block, cache.dtype),
            pltpu.VMEM((2 * count,) + block, cache.dtype),
            pltpu.VMEM((RING * K,) + block, cache.dtype),
            pltpu.VMEM((RING * K,) + block, cache.dtype),
            dma((tensors - 1, pieces)),
            dma((tensors - 1, pieces)),
        ]
        + [dma((pieces,))] * 4
        + flow
        + flow,
        compiler_params=pltpu.CompilerParams(
            collective_id=collective, has_side_effects=True, vmem_limit_bytes=62 * 2**20
        ),
    )(table, cache)


def attend_kernel(nodes, kv_dev, group_q, tab_ref, q_ref, fresh_ref, *refs):
    kv_refs = refs[:STEP_BLOCKS]
    out_ref, q_s, m_s, l_s, acc_s = refs[STEP_BLOCKS:]
    i = pl.program_id(0)
    factor = math.log2(math.e) / math.sqrt(HD)
    rows = group_q * NODE_TOK
    tile = min(rows, 256)
    contract = (((1,), (1,)), ((), ()))

    @pl.when(i == 0)
    def _():
        row = lax.broadcasted_iota(jnp.int32, (tile, NODE_TOK), 0) & (NODE_TOK - 1)
        col = lax.broadcasted_iota(jnp.int32, (tile, NODE_TOK), 1)
        causal = col <= row
        for n in range(nodes):
            tok = slice(n * NODE_TOK, (n + 1) * NODE_TOK)
            for h in range(kv_dev):
                k = fresh_ref[tok, h * 2 * HD : h * 2 * HD + HD]
                v = fresh_ref[tok, h * 2 * HD + HD : (h + 1) * 2 * HD]
                kk = jnp.concatenate([k, k], axis=1)
                vv = jnp.concatenate([v, jnp.ones_like(v)], axis=1)
                p = n * kv_dev + h
                for a in range(group_q):
                    head = h * group_q + a
                    here = slice(a * NODE_TOK, (a + 1) * NODE_TOK)
                    wide_q = q_ref[tok, head * HD : (head + 1) * HD].astype(jnp.float32) * factor
                    upper = wide_q.astype(jnp.bfloat16)
                    q_s[p, here, :HD] = upper
                    q_s[p, here, HD:] = (wide_q - upper.astype(jnp.float32)).astype(jnp.bfloat16)
                for start in range(0, rows, tile):
                    here = slice(start, start + tile)
                    s = lax.dot_general(
                        q_s[p, here, :], kk, contract, preferred_element_type=jnp.float32
                    )
                    s = jnp.where(causal, s, -jnp.inf)
                    m = jnp.max(s, axis=1, keepdims=True)
                    w = jnp.exp2(s - m)
                    m_s[p, here, :] = jnp.broadcast_to(m, (tile, 128))
                    both = jnp.dot(w.astype(jnp.bfloat16), vv, preferred_element_type=jnp.float32)
                    acc_s[p, here, :] = both[:, :HD]
                    l_s[p, here, :] = both[:, HD:]

    def visit(n, masked):
        keys = STEP_BLOCKS * BT
        if masked:
            slot = lax.broadcasted_iota(jnp.int32, (1, keys), 1) // BT + i * STEP_BLOCKS
            seen = slot < tab_ref[5, n]
        for h in range(kv_dev):
            k = jnp.concatenate([r[0, :, h * 2 * HD : h * 2 * HD + HD] for r in kv_refs], axis=0)
            v = jnp.concatenate([r[0, :, h * 2 * HD + HD : (h + 1) * 2 * HD] for r in kv_refs], axis=0)
            vv = jnp.concatenate([v, jnp.ones_like(v)], axis=1)
            kk = jnp.concatenate([k, k], axis=1)
            p = n * kv_dev + h
            for start in range(0, rows, tile):
                here = slice(start, start + tile)
                s = lax.dot_general(
                    q_s[p, here, :], kk, contract, preferred_element_type=jnp.float32
                )
                if masked:
                    s = jnp.where(seen, s, -jnp.inf)
                m_old = m_s[p, here, :]
                m_new = jnp.maximum(m_old, jnp.max(s, axis=1, keepdims=True))
                alpha = jnp.exp2(m_old - m_new)
                w = [jnp.exp2(s[:, u * 128 : (u + 1) * 128] - m_new) for u in range(keys // 128)]
                wide = jnp.concatenate([x.astype(jnp.bfloat16) for x in w], axis=1)
                both = jnp.dot(wide, vv, preferred_element_type=jnp.float32)
                acc_s[p, here, :] = acc_s[p, here, :] * alpha + both[:, :HD]
                l_s[p, here, :] = l_s[p, here, :] * alpha + both[:, HD:]
                m_s[p, here, :] = m_new

    for n in range(nodes):
        first = i * STEP_BLOCKS
        whole = first + STEP_BLOCKS <= tab_ref[5, n]

        @pl.when(whole)
        def _():
            visit(n, False)

        @pl.when(jnp.logical_and(first < tab_ref[5, n], jnp.logical_not(whole)))
        def _():
            visit(n, True)

    @pl.when(i == pl.num_programs(0) - 1)
    def _():
        for n in range(nodes):
            for h in range(kv_dev):
                p = n * kv_dev + h
                for a in range(group_q):
                    head = h * group_q + a
                    here = slice(a * NODE_TOK, (a + 1) * NODE_TOK)
                    total = l_s[p, here, :]
                    out_ref[n * NODE_TOK : (n + 1) * NODE_TOK, head * HD : (head + 1) * HD] = (
                        acc_s[p, here, :] / total
                    ).astype(out_ref.dtype)


def attend(queries, fresh, blocks, table, nodes, kv_dev, group_q):
    new_rows, q_cols = queries.shape
    width = blocks.shape[2]
    rows = group_q * NODE_TOK
    pairs = nodes * kv_dev

    def kv_spec(u):
        return pl.BlockSpec((1, BT, width), lambda i, tab: (tab[3, i * STEP_BLOCKS + u], 0, 0))

    return pl.pallas_call(
        functools.partial(attend_kernel, nodes, kv_dev, group_q),
        out_shape=jax.ShapeDtypeStruct((new_rows, q_cols), queries.dtype),
        grid_spec=pltpu.PrefetchScalarGridSpec(
            num_scalar_prefetch=1,
            grid=(P_SIZE // STEP_BLOCKS,),
            in_specs=[
                pl.BlockSpec((new_rows, q_cols), lambda i, tab: (0, 0)),
                pl.BlockSpec((new_rows, width), lambda i, tab: (0, 0)),
            ]
            + [kv_spec(u) for u in range(STEP_BLOCKS)],
            out_specs=pl.BlockSpec((new_rows, q_cols), lambda i, tab: (0, 0)),
            scratch_shapes=[
                pltpu.VMEM((pairs, rows, 2 * HD), jnp.bfloat16),
                pltpu.VMEM((pairs, rows, 128), jnp.float32),
                pltpu.VMEM((pairs, rows, 128), jnp.float32),
                pltpu.VMEM((pairs, rows, HD), jnp.float32),
            ],
        ),
        compiler_params=pltpu.CompilerParams(vmem_limit_bytes=48 * 2**20),
    )(table, queries, fresh, *([blocks] * STEP_BLOCKS))


def body(queries, new_kv, cache, parents, depth):
    tensor_size = lax.axis_size("tensor")
    branches = lax.axis_size("branch")
    tensor_pos = lax.axis_index("tensor")
    branch_pos = lax.axis_index("branch")
    sharing = HQ // KVH
    heads_dev = queries.shape[1] // HD
    kv_dev = max(1, heads_dev // sharing)
    group_q = heads_dev // kv_dev
    first_kv = tensor_pos * heads_dev // sharing
    blk_dev = cache.shape[0]
    new_rows = queries.shape[0]
    width = kv_dev * 2 * HD
    nodes = depth.shape[1]
    zs = branches // 2
    first_cols = [(t * heads_dev // sharing) * 2 * HD for t in range(tensor_size)]
    fresh = lax.dynamic_slice_in_dim(new_kv, first_kv, kv_dev, 1).reshape(new_rows, width)
    out_blocks = (branches * blk_dev // 2, 2, tensor_size, cache.shape[1], width)

    def flood(cache, picks, collective):
        packed = pack(cache, picks, blk_dev, first_cols, width)
        return spread(packed, branches, blk_dev, collective).reshape(out_blocks)

    region = (branches * blk_dev - 2 * blk_dev) // 4
    every = jnp.arange(blk_dev, dtype=jnp.int32)
    if zs <= 4 and blk_dev % (2 * K) == 0 and region >= LEVELS[-1] and branches * blk_dev <= 256:
        table = make_plan(parents, depth, branches, blk_dev, region)

        def with_count(count, collective):
            def run(table, cache):
                return relay(
                    table, cache, zs, tensor_size, count, region, first_cols, width, collective
                )

            return run

        runs = [with_count(count, 1 + i) for i, count in enumerate(LEVELS)]
        runs.append(lambda table, cache: flood(cache, every, 1 + len(LEVELS)))
        gathered = lax.switch(table[4, 0], runs, table, cache)
    else:
        own_row = lax.dynamic_index_in_dim(parents, branch_pos, 0, keepdims=False)
        own_row = own_row[jnp.minimum(jnp.arange(P_SIZE), jnp.max(depth[0]) - 1)]
        filler = jnp.zeros((128,), jnp.int32)
        rows = [filler] * 3 + [filler.at[:P_SIZE].set(own_row), filler, filler.at[:nodes].set(depth[0])]
        table = jnp.stack(rows + [filler] * 2)
        gathered = flood(cache, every, 1)
    blocks = gathered.reshape(branches * blk_dev, BT, width)
    return attend(queries, fresh, blocks, table, nodes, kv_dev, group_q)


def solution(mesh):
    placed = (
        P("branch", "tensor"),
        P("branch", None, None),
        P("branch", "tensor", None),
        P(),
        P("branch", None),
    )
    return jax.shard_map(
        body, mesh=mesh, in_specs=placed, out_specs=P("branch", "tensor"), check_vma=False
    )
```
